32 devices in a mesh: row: 16 (over z, y, x), wt: 2 (over core).
Axes of the slice: x: 2, y: 2, z: 4, core: 2. Of those that a mesh axis runs over, the one named last changes fastest.
Arguments:
- atoms: bfloat16 [2, 2048, 768], P('wt', 'row'), may hold values from -6 to 6
- coords: bfloat16 [3, 2, 2048], P(None, 'wt', 'row'), may hold values from -8 to 8
- atom_types: int32 [2, 2048], P('wt', 'row'), may hold values from 0 to 127
- lengths: int32 [2, 16], P('wt'), may hold values from 1 to 1024, 2048 in all within a row
- times: float32 [2], P('wt'), may hold values from 0.05 to 1
- type_table: bfloat16 [128, 768], replicated, may hold values from -3 to 3
- gain_one: float32 [768], replicated, may hold values from 0.5 to 1.5
- shift_one: float32 [768], replicated, may hold values from -1 to 1
- w_qkv: bfloat16 [768, 2304], P('wt'), may hold values from -0.21875 to 0.21875
- centers: float32 [128], replicated, may hold values from 0 to 12
- widths: float32 [128], replicated, may hold values from 0.05 to 120
- w_pair: bfloat16 [128, 32], replicated, may hold values from -460 to 460
- w_out: bfloat16 [768, 768], P('wt'), may hold values from -0.875 to 0.875
- gain_two: float32 [768], replicated, may hold values from 0.5 to 1.5
- shift_two: float32 [768], replicated, may hold values from -1 to 1
- w_up: bfloat16 [768, 3072], P('wt'), may hold values from -0.21875 to 0.21875
- w_down: bfloat16 [3072, 768], P('wt'), may hold values from -0.109375 to 0.109375
- w_force: bfloat16 [3, 768], replicated, may hold values from -0.21875 to 0.21875
- out_grad: bfloat16 [2, 2048, 768], P('wt', 'row'), may hold values from -6 to 6
- force_grad: float32 [3, 2, 2048], P(None, 'wt', 'row'), may hold values from -6 to 6
Outputs:
- block_out: bfloat16 [2, 2048, 768], P('wt', 'row')
- forces: float32 [3, 2, 2048], P(None, 'wt', 'row')
- atoms_grad: float32 [2, 2048, 768], P('wt', 'row')
- type_table_grad: float32 [128, 768], replicated
- gain_one_grad: float32 [768], replicated
- shift_one_grad: float32 [768], replicated
- w_qkv_grad: float32 [768, 2304], P('wt', 'row')
- centers_grad: float32 [128], replicated
- widths_grad: float32 [128], replicated
- w_pair_grad: float32 [128, 32], replicated
- w_out_grad: float32 [768, 768], P('wt', 'row')
- gain_two_grad: float32 [768], replicated
- shift_two_grad: float32 [768], replicated
- w_up_grad: float32 [768, 3072], P('wt', 'row')
- w_down_grad: float32 [3072, 768], P('wt', 'row')
- w_force_grad: float32 [3, 768], replicated
The draws below stay inside these ranges and needn't reach their ends.
Inputs may be any that keep to these rules, and one draw needn't show every extreme that they name: Each micro-batch's molecules fill its 2048 positions in order, their lengths summing to 2048; some molecule has exactly 1024 atoms.
All inputs are finite; a program needn't handle non-finite values.
Results may differ from the reference program's by a relative error of at most 0.019.
Values may be sent and summed in bfloat16 or wider, within the bound.
A program may use at most 192 MiB of HBM per device.

```python
import math
import jax
import jax.numpy as jnp
import numpy as np
from jax import lax

D = 768
HEADS = 32
HDIM = 24
FF = 3072
KERN = 128
NTYPES = 128
MAXLEN = 1024
TOK_MB = 2048
MB = 2
ITEMS = 16


def kernel_plan(key):
    wide_count = max(4, KERN // 8)
    kern_order = jax.random.permutation(jax.random.fold_in(key, 11), KERN)
    is_wide = kern_order < wide_count
    narrow_width = jnp.exp(jax.random.uniform(jax.random.fold_in(key, 12), (KERN,), jnp.float32, math.log(0.05), math.log(0.25)))
    broad_width = jnp.exp(jax.random.uniform(jax.random.fold_in(key, 13), (KERN,), jnp.float32, math.log(60.0), math.log(120.0)))
    chosen = jnp.clip(jnp.where(is_wide, broad_width, narrow_width), 0.05, 120.0)
    return (chosen, is_wide)


def draw_widths(key, part):
    return kernel_plan(key)[0].astype(jnp.float32)


def draw_w_pair(key, part):
    chosen, is_wide = kernel_plan(key)
    broad_base = jnp.clip(jax.random.normal(jax.random.fold_in(key, 15), (KERN, HEADS), jnp.float32), -3.0, 3.0)
    broad_rows = 0.5 * broad_base * math.sqrt(2.0 * math.pi) * chosen[:, None]
    narrow_rows = jnp.clip(0.3 * jax.random.normal(jax.random.fold_in(key, 16), (KERN, HEADS), jnp.float32), -1.2, 1.2)
    return jnp.where(is_wide[:, None], broad_rows, narrow_rows).astype(jnp.bfloat16)


def set_ends(result, key, smallest, high):
    index_at = [jax.random.randint(jax.random.fold_in(key, axis), (), 0, length) for axis, length in enumerate(result.shape)]
    widest = result.shape.index(max(result.shape))
    next_to = index_at[:widest] + [(index_at[widest] + 1) % result.shape[widest]] + index_at[widest + 1:]
    return result.at[tuple(index_at)].set(smallest).at[tuple(next_to)].set(high)


def level_of(key, extent, pieces, least, high):
    def one(dim, shards_of):
        steps = jax.random.uniform(jax.random.fold_in(jax.random.fold_in(key, 6), dim), (shards_of,), jnp.float32, least / len(pieces), high / len(pieces))
        return jnp.repeat(jnp.exp(steps), extent[dim] // shards_of).reshape((-1,) + (1,) * (len(extent) - dim - 1))

    level = one(*pieces[0])
    for cut in pieces[1:]:
        level = level * one(*cut)
    return level


def profile(count, total, reach, slope):
    weights = [(1 << 20) // math.isqrt(standing ** slope) + 1 for standing in range(2, count + 1)]
    rest, given = total - reach - (count - 1), [1] * (count - 1)
    while rest > 0:
        candidates = [i for i in range(count - 1) if given[i] < reach]
        pool, remaining = sum([weights[i] for i in candidates]), rest
        for i in candidates:
            more = min(reach - given[i], max(1, remaining * weights[i] // pool), rest)
            given[i] = given[i] + more
            rest = rest - more
    return np.array([reach] + given)


def uneven(key, count, total, most, slope):
    if count == 2:
        one = jax.random.randint(key, (), max(1, total - most), min(most, total - 1) + 1)
        return jnp.stack([one, total - one])
    sizes = jnp.asarray(profile(count, total, most, slope), jnp.int32)
    twos = (count - 1) // 2
    giver, taker = sizes[1:1 + 2 * twos:2], sizes[2:2 + 2 * twos:2]
    slack = jnp.minimum(giver - 1, most - taker)
    passed = jax.random.randint(jax.random.fold_in(key, 1), (twos,), 0, 1 << 20) % (slack + 1)
    sizes = sizes.at[1:1 + 2 * twos:2].set(giver - passed).at[2:2 + 2 * twos:2].set(taker + passed)
    return sizes[jax.random.permutation(jax.random.fold_in(key, 2), count)]


def normal_values(own_key, dims, deviation, limit, split=(), held_as=jnp.bfloat16):
    entries = deviation * jax.random.normal(own_key, dims, jnp.float32)
    if split:
        entries = entries * level_of(own_key, dims, split, -0.22, 0.18)
    return jnp.clip(entries, -limit, limit).astype(held_as)


def setup_inputs(seed: int = 0) -> dict:
    key_list = jax.random.split(jax.random.key(seed), 21)
    return {
        "atoms": normal_values(key_list[0], (MB, TOK_MB, D), 1.0, 6.0, ((0, 2), (1, 16))),
        "coords": normal_values(key_list[1], (3, MB, TOK_MB), 2.0, 8.0, ((1, 2), (2, 16))),
        "atom_types": set_ends(jax.random.randint(key_list[2], (MB, TOK_MB), 0, NTYPES), jax.random.fold_in(key_list[2], 1), 0, NTYPES - 1).astype(jnp.int32),
        "lengths": jax.vmap(lambda own: uneven(own, ITEMS, TOK_MB, MAXLEN, 2))(jax.random.split(key_list[3], MB)).reshape((MB, ITEMS)).astype(jnp.int32),
        "times": jnp.clip(0.05 + 0.95 * jax.random.uniform(key_list[4], (MB,), jnp.float32) ** level_of(key_list[4], (MB,), ((0, 2),), -0.2, 0.2), 0.05, 1.0),
        "type_table": normal_values(key_list[5], (NTYPES, D), 0.5, 3.0),
        "gain_one": jnp.clip(1.0 + 0.1 * jax.random.normal(key_list[6], (D,), jnp.float32), 0.5, 1.5),
        "shift_one": normal_values(key_list[7], (D,), 0.2, 1.0, (), jnp.float32),
        "w_qkv": normal_values(key_list[8], (D, 3 * D), D ** -0.5, 0.21875, ((0, 2),)),
        "centers": jnp.clip(jax.random.uniform(key_list[9], (KERN,), jnp.float32, 0.0, 12.0), 0.0, 12.0),
        "widths": draw_widths(jax.random.fold_in(key_list[20], 71), 0),
        "w_pair": draw_w_pair(jax.random.fold_in(key_list[20], 71), 0),
        "w_out": normal_values(key_list[12], (D, D), (D // 16) ** -0.5, 0.875, ((0, 2),)),
        "gain_two": jnp.clip(1.0 + 0.1 * jax.random.normal(key_list[13], (D,), jnp.float32), 0.5, 1.5),
        "shift_two": normal_values(key_list[14], (D,), 0.2, 1.0, (), jnp.float32),
        "w_up": normal_values(key_list[15], (D, FF), D ** -0.5, 0.21875, ((0, 2),)),
        "w_down": normal_values(key_list[16], (FF, D), FF ** -0.5, 0.109375, ((0, 2),)),
        "w_force": normal_values(key_list[17], (3, D), D ** -0.5, 0.21875),
        "out_grad": normal_values(key_list[18], (MB, TOK_MB, D), 1.0, 6.0, ((0, 2), (1, 16))),
        "force_grad": normal_values(key_list[19], (3, MB, TOK_MB), 1.0, 6.0, ((1, 2), (2, 16)), jnp.float32),
    }


@jax.custom_vjp
def low(v):
    return lax.optimization_barrier(v.astype(jnp.bfloat16)).astype(jnp.float32)

@jax.custom_vjp
def low_back(v):
    return v

def low_keep(v):
    return (low(v), None)

def low_pass(kept, grad):
    return (grad,)

def back_keep(v):
    return (v, None)

def back_low(kept, grad):
    return (low(grad),)
low.defvjp(low_keep, low_pass)
low_back.defvjp(back_keep, back_low)
NEG_FILL = -1e+30
HIGHEST = lax.Precision.HIGHEST

def product(left_side, right_side):
    return jnp.dot(left_side, right_side, precision=HIGHEST, preferred_element_type=jnp.float32)

def layer_norm(values_in, gain_vec, shift_vec):
    average = lax.optimization_barrier(jnp.mean(values_in, axis=-1, keepdims=True))
    centred = values_in - average
    inverse = lax.rsqrt(lax.optimization_barrier(jnp.mean(centred * centred, axis=-1, keepdims=True)) + 1e-05)
    return centred * inverse * gain_vec + shift_vec

def gelu_tanh(values_in):
    return 0.5 * values_in * (1.0 + jnp.tanh(0.7978845608028654 * (values_in + 0.044715 * values_in * values_in * values_in)))

def time_code(moment, model_width):
    half_width = model_width // 2
    frequency = jnp.exp(-math.log(10000.0) * jnp.arange(half_width, dtype=jnp.float32) / half_width)
    angles = 100.0 * moment * frequency
    return jnp.concatenate([jnp.sin(angles), jnp.cos(angles)])

def item_ids(places, item_ends):
    return lax.optimization_barrier(jnp.sum((places[:, None] >= item_ends[None, :]).astype(jnp.int32), axis=1))

def kernel_terms(query_pos, key_pos, centers, widths):
    differ = query_pos[:, :, None] - key_pos[:, None, :]
    distance = jnp.sqrt(lax.optimization_barrier(jnp.sum(differ * differ, axis=0)))
    scaled_gap = (distance[:, :, None] - centers) / widths
    return (scaled_gap, jnp.exp(-0.5 * scaled_gap * scaled_gap) / (math.sqrt(2.0 * math.pi) * widths))

def attend(queries, keys_in, values_in, positions, item_index, centers, widths, w_pair):
    all_rows = queries.shape[0]
    query_block = min(256, all_rows)
    window = min(all_rows, query_block + 2 * MAXLEN)
    score_scale = HDIM ** (-0.5)

    def one_block(first_row):
        window_start = jnp.clip(first_row - MAXLEN, 0, all_rows - window).astype(jnp.int32)
        block_q = lax.dynamic_slice_in_dim(queries, first_row, query_block, 0).reshape(query_block, HEADS, HDIM)
        block_k = lax.dynamic_slice_in_dim(keys_in, window_start, window, 0).reshape(window, HEADS, HDIM)
        block_v = lax.dynamic_slice_in_dim(values_in, window_start, window, 0).reshape(window, HEADS, HDIM)
        query_pos = lax.dynamic_slice_in_dim(positions, first_row, query_block, 1)
        key_pos = lax.dynamic_slice_in_dim(positions, window_start, window, 1)
        query_items = lax.dynamic_slice_in_dim(item_index, first_row, query_block, 0)
        key_items = lax.dynamic_slice_in_dim(item_index, window_start, window, 0)
        scaled_gap, kernel = kernel_terms(query_pos, key_pos, centers, widths)
        pair_bias = jnp.einsum('qkc,ch->hqk', low(kernel), w_pair, precision=HIGHEST)
        logits = low_back(score_scale * jnp.einsum('qhd,khd->hqk', block_q, block_k, precision=HIGHEST) + pair_bias)
        same_item = (query_items[:, None] == key_items[None, :])[None, :, :]
        logits = jnp.where(same_item, logits, NEG_FILL)
        row_top = lax.optimization_barrier(jnp.max(logits, axis=-1, keepdims=True))
        exponent = jnp.exp(logits - row_top)
        weights = exponent / lax.optimization_barrier(jnp.sum(exponent, axis=-1, keepdims=True))
        mixed = jnp.einsum('hqk,khd->qhd', weights, block_v, precision=HIGHEST)
        return mixed.reshape(query_block, HEADS * HDIM)
    starts = jnp.arange(all_rows // query_block, dtype=jnp.int32) * query_block
    return lax.map(jax.checkpoint(one_block), starts).reshape(all_rows, HEADS * HDIM)

def reference(atoms, coords, atom_types, lengths, times, type_table, gain_one, shift_one, w_qkv, centers, widths, w_pair, w_out, gain_two, shift_two, w_up, w_down, w_force, out_grad, force_grad):
    places = jnp.arange(TOK_MB, dtype=jnp.int32)
    item_ends = jnp.cumsum(lengths, axis=1).astype(jnp.int32)
    type_codes = jnp.arange(NTYPES, dtype=jnp.int32)
    item_list = [item_ids(places, item_ends[micro]) for micro in range(MB)]
    onehot_list = [(atom_types[micro][:, None] == type_codes[None, :]).astype(jnp.float32) for micro in range(MB)]
    positions = coords.astype(jnp.float32)

    def forward(atoms_in, table_in, gain_a, shift_a, qkv_in, centers_in, widths_in, pair_in, out_in, gain_b, shift_b, up_in, down_in, force_in):
        sums_list, force_list = ([], [])
        for micro in range(MB):
            base_rows = atoms_in[micro] + time_code(times[micro], D) + product(onehot_list[micro], table_in)
            normed_in = low(layer_norm(base_rows, gain_a, shift_a))
            qkv_rows = low(low_back(product(normed_in, qkv_in)))
            attended = attend(qkv_rows[:, :D], qkv_rows[:, D:2 * D], qkv_rows[:, 2 * D:], positions[:, micro, :], item_list[micro], centers_in, widths_in, pair_in)
            att_low = low(low_back(attended))
            after_att = base_rows + low_back(product(att_low, out_in))
            ffn_in = low(layer_norm(after_att, gain_b, shift_b))
            activated = low(low_back(gelu_tanh(low_back(product(ffn_in, up_in)))))
            block_sum = after_att + low_back(product(activated, down_in))
            sums_list.append(block_sum)
            force_list.append(product(force_in, low(block_sum).T))
        return (jnp.stack(sums_list), jnp.stack(force_list, axis=1))
    primals = (atoms.astype(jnp.float32), type_table.astype(jnp.float32), gain_one, shift_one, w_qkv.astype(jnp.float32), centers, widths, w_pair.astype(jnp.float32), w_out.astype(jnp.float32), gain_two, shift_two, w_up.astype(jnp.float32), w_down.astype(jnp.float32), w_force.astype(jnp.float32))
    (block_sums, forces), pullback = jax.vjp(forward, *primals)
    grads = pullback((out_grad.astype(jnp.float32), force_grad))
    return (block_sums.astype(jnp.bfloat16), forces, grads[0], grads[1], grads[2], grads[3], grads[4], grads[5], grads[6], grads[7], grads[8], grads[9], grads[10], grads[11], grads[12], grads[13])
```

```python
import functools
import math

import jax
import jax.numpy as jnp
from jax import lax
from jax.experimental import pallas as pl
from jax.experimental.pallas import tpu as pltpu
from jax.sharding import PartitionSpec as P

MAXLEN = 1024
NEG_FILL = -1e30
HIGHEST = lax.Precision.HIGHEST
QB = 32
TILE = 128
HG = 8
GW = 256
LOG2E = 1.4426950408889634
bf16 = jnp.bfloat16
f32 = jnp.float32


def shifted(x, axis, by):
    length = lax.axis_size(axis)
    pairs = [(i, i + by) for i in range(length) if 0 <= i + by < length]
    return lax.ppermute(x, axis, pairs)


def swap_cores(x):
    return lax.ppermute(x, "wt", [(0, 1), (1, 0)])


def norm_parts(values_in):
    average = jnp.mean(values_in, axis=-1, keepdims=True)
    centred = values_in - average
    inverse = lax.rsqrt(jnp.mean(centred * centred, axis=-1, keepdims=True) + 1e-05)
    return (centred * inverse, inverse)


def norm_back(grad_out, normed, inverse, gain_vec):
    grad_normed = grad_out * gain_vec
    mean_grad = jnp.mean(grad_normed, axis=-1, keepdims=True)
    mean_mixed = jnp.mean(grad_normed * normed, axis=-1, keepdims=True)
    grad_in = inverse * (grad_normed - mean_grad - normed * mean_mixed)
    return (grad_in, jnp.sum(grad_out * normed, axis=0), jnp.sum(grad_out, axis=0))


def gelu_tanh(values_in):
    return (
        0.5
        * values_in
        * (
            1.0
            + jnp.tanh(
                0.7978845608028654 * (values_in + 0.044715 * values_in * values_in * values_in)
            )
        )
    )


def time_code(moment, model_width):
    half_width = model_width // 2
    frequency = jnp.exp(-math.log(10000.0) * jnp.arange(half_width, dtype=jnp.float32) / half_width)
    angles = 100.0 * moment * frequency
    return jnp.concatenate([jnp.sin(angles), jnp.cos(angles)])


def item_ids(places, item_ends):
    return jnp.sum((places[:, None] >= item_ends[None, :]).astype(jnp.int32), axis=1)


def cross_rows(left_side, right_side):
    return lax.dot_general(
        left_side, right_side, (((0,), (0,)), ((), ())), preferred_element_type=jnp.float32
    )


def along_rows(left_side, right_side):
    return lax.dot_general(
        left_side, right_side, (((1,), (1,)), ((), ())), preferred_element_type=jnp.float32
    )


def head_mask(groups_dim):
    h = lax.broadcasted_iota(jnp.int32, (HG, GW), 0)
    f = lax.broadcasted_iota(jnp.int32, (HG, GW), 1)
    lo = h * groups_dim
    return (f >= lo) & (f < lo + groups_dim)


def expand(rows, mask):
    parts = [
        jnp.where(mask, jnp.broadcast_to(rows[i : i + 1, :], (HG, GW)), 0.0)
        for i in range(rows.shape[0])
    ]
    return jnp.concatenate(parts, axis=0)


def collapse(stacked, mask):
    count = stacked.shape[0] // HG
    parts = [
        jnp.sum(jnp.where(mask, stacked[i * HG : (i + 1) * HG, :], 0.0), axis=0, keepdims=True)
        for i in range(count)
    ]
    return jnp.concatenate(parts, axis=0)


def tile_distance(qpos_ref, kpos_ref, tile):
    total = None
    for axis in range(3):
        differ = qpos_ref[:, axis : axis + 1] - kpos_ref[tile, axis : axis + 1, :]
        total = differ * differ if total is None else total + differ * differ
    return jnp.sqrt(total)


def fwd_kernel(
    head_dim, lo_ref, hi_ref, q_ref, kt_ref, v_ref, qpos_ref, kpos_ref, qid_ref, kid_ref,
    cen_ref, amp_ref, lnorm_ref, wpt_ref, p_ref, o_ref, rl_ref,
    qexp, score, top, dist, neg, kern, bias, acc, total,
):
    block = pl.program_id(0)
    lo, hi = lo_ref[block], hi_ref[block]
    groups = wpt_ref.shape[0] // HG
    rows = QB * HG
    scale = head_dim ** (-0.5)
    mask = head_mask(head_dim)
    for g in range(groups):
        qexp[g] = expand(q_ref[:, g * GW : (g + 1) * GW].astype(f32), mask).astype(bf16)
        acc[g] = jnp.zeros((rows, GW), f32)
    top[...] = jnp.full(top.shape, NEG_FILL, f32)
    total[...] = jnp.zeros(total.shape, f32)

    def first(tile, carry):
        dist[...] = tile_distance(qpos_ref, kpos_ref, tile)
        neg[...] = jnp.where(qid_ref[:, 0:1] == kid_ref[tile], 0.0, NEG_FILL)

        def some_kernels(cg, carry):
            at = pl.ds(pl.multiple_of(cg * 16, 16), 16)
            cen, amp, lnorm = cen_ref[at, :], amp_ref[at, :], lnorm_ref[at, :]
            for i in range(QB):
                t = (dist[i : i + 1, :] - cen) * amp
                kern[at, i * TILE : (i + 1) * TILE] = jnp.exp2(lnorm - t * t).astype(bf16)
            return carry

        lax.fori_loop(0, cen_ref.shape[0] // 16, some_kernels, 0)
        for part in range(QB // 8):
            at = slice(part * 8 * TILE, (part + 1) * 8 * TILE)
            bias[:, at] = jnp.dot(wpt_ref[...], kern[:, at], preferred_element_type=f32)
        for g in range(groups):
            dots = jnp.dot(qexp[g], kt_ref[tile, g * GW : (g + 1) * GW, :], preferred_element_type=f32)
            for i in range(QB):
                here = slice(g * rows + i * HG, g * rows + (i + 1) * HG)
                value = (
                    dots[i * HG : (i + 1) * HG, :] * scale
                    + bias[g * HG : (g + 1) * HG, i * TILE : (i + 1) * TILE]
                    + neg[i : i + 1, :]
                )
                score[tile, here, :] = value
                top[here, :] = jnp.maximum(top[here, :], value)
        return carry

    lax.fori_loop(lo, hi, first, 0)
    top[...] = jnp.broadcast_to(jnp.max(top[...], axis=1, keepdims=True), top.shape)

    def second(tile, carry):
        for g in range(groups):
            here = slice(g * rows, (g + 1) * rows)
            prob = jnp.exp(score[tile, here, :] - top[here, :])
            total[here, :] += prob
            low = prob.astype(bf16)
            p_ref[0, tile, here, :] = low
            acc[g] += jnp.dot(low, v_ref[tile, :, g * GW : (g + 1) * GW], preferred_element_type=f32)
        return carry

    lax.fori_loop(lo, hi, second, 0)
    for g in range(groups):
        here = slice(g * rows, (g + 1) * rows)
        inverse = 1.0 / jnp.sum(total[here, :], axis=1, keepdims=True)
        rl_ref[here, :] = jnp.broadcast_to(inverse, (rows, TILE))
        o_ref[:, g * GW : (g + 1) * GW] = collapse(acc[g] * inverse, mask)


def bwd_kernel(
    head_dim, lo_ref, hi_ref, p_ref, rl_ref, q_ref, do_ref, o_ref, k_ref, vt_ref, qpos_ref, kpos_ref,
    cen_ref, amp_ref, lnorm_ref, wp_ref, dq_ref, dkt_ref, dvt_ref, m0_ref, sums_ref,
    qext, doexp, doext, delta, dqacc, glow, dist, kern, gk,
):
    block = pl.program_id(0)
    lo, hi = lo_ref[block], hi_ref[block]
    groups = q_ref.shape[1] // GW
    rows = QB * HG
    mask = head_mask(head_dim)

    @pl.when(block == 0)
    def _():
        dkt_ref[...] = jnp.zeros(dkt_ref.shape, f32)
        dvt_ref[...] = jnp.zeros(dvt_ref.shape, f32)
        m0_ref[...] = jnp.zeros(m0_ref.shape, f32)
        sums_ref[...] = jnp.zeros(sums_ref.shape, f32)

    for g in range(groups):
        lanes = slice(g * GW, (g + 1) * GW)
        here = slice(g * rows, (g + 1) * rows)
        inverse = rl_ref[here, 0:1]
        qext[g] = jnp.transpose(expand(q_ref[:, lanes].astype(f32), mask)).astype(bf16)
        grads = do_ref[:, lanes].astype(f32)
        both = expand(grads, mask) * inverse
        doexp[g] = both.astype(bf16)
        doext[g] = jnp.transpose(both).astype(bf16)
        mixed = jnp.sum(expand(grads * o_ref[:, lanes], mask), axis=1, keepdims=True) * inverse
        delta[here, :] = jnp.broadcast_to(mixed, (rows, TILE))
        dqacc[g] = jnp.zeros((rows, GW), f32)

    def one_tile(tile, carry):
        dist[...] = tile_distance(qpos_ref, kpos_ref, tile)
        for pair in range(groups // 2):
            grads = []
            for g in (2 * pair, 2 * pair + 1):
                lanes = slice(g * GW, (g + 1) * GW)
                here = slice(g * rows, (g + 1) * rows)
                low = p_ref[0, tile, here, :]
                dp = jnp.dot(doexp[g], vt_ref[tile, lanes, :], preferred_element_type=f32)
                gl = low.astype(f32) * (dp - delta[here, :])
                grads.append(gl)
                gl_low = gl.astype(bf16)
                dqacc[g] += jnp.dot(gl_low, k_ref[tile, :, lanes], preferred_element_type=f32)
                dkt_ref[tile, lanes, :] += jnp.dot(qext[g], gl_low, preferred_element_type=f32)
                dvt_ref[tile, lanes, :] += jnp.dot(doext[g], low, preferred_element_type=f32)
            for i in range(QB):
                at = slice(i * HG, (i + 1) * HG)
                glow[pair * 16 : (pair + 1) * 16, i * TILE : (i + 1) * TILE] = jnp.concatenate(
                    [grads[0][at, :], grads[1][at, :]], axis=0
                ).astype(bf16)
        for part in range(QB // 8):
            at = slice(part * 8 * TILE, (part + 1) * 8 * TILE)
            gk[:, at] = jnp.dot(wp_ref[...], glow[:, at], preferred_element_type=f32)

        def some_kernels(cg, carry):
            at = pl.ds(pl.multiple_of(cg * 16, 16), 16)
            cen, amp, lnorm = cen_ref[at, :], amp_ref[at, :], lnorm_ref[at, :]
            plain = jnp.zeros((16, TILE), f32)
            once = jnp.zeros((16, TILE), f32)
            twice = jnp.zeros((16, TILE), f32)
            for i in range(QB):
                lanes = slice(i * TILE, (i + 1) * TILE)
                t = (dist[i : i + 1, :] - cen) * amp
                value = jnp.exp2(lnorm - t * t)
                kern[at, lanes] = value.astype(bf16)
                weighted = gk[at, lanes] * value
                plain = plain + weighted
                weighted = weighted * t
                once = once + weighted
                twice = twice + weighted * t
            sums_ref[0, at, :] += plain
            sums_ref[1, at, :] += once
            sums_ref[2, at, :] += twice
            return carry

        lax.fori_loop(0, cen_ref.shape[0] // 16, some_kernels, 0)
        m0_ref[...] += lax.dot_general(
            glow[...], kern[...], (((1,), (1,)), ((), ())), preferred_element_type=f32
        )
        return carry

    lax.fori_loop(lo, hi, one_tile, 0)
    for g in range(groups):
        dq_ref[:, g * GW : (g + 1) * GW] = collapse(dqacc[g], mask)


def whole(shape):
    return pl.BlockSpec(shape, lambda *_: (0,) * len(shape), pipeline_mode=pl.Buffered(1))


def attention_forward(lo, hi, q, kt, v, qpos, kpos, qid, kid, cen, amp, lnorm, wpt, head_dim):
    tiles = kt.shape[0]
    wide = q.shape[1]
    groups = wide // GW
    rows = QB * HG
    blocks = q.shape[0] // QB
    kernels, heads = cen.shape[0], wpt.shape[0]
    by_block = lambda b, *_: (b, 0)
    return pl.pallas_call(
        functools.partial(fwd_kernel, head_dim),
        grid_spec=pltpu.PrefetchScalarGridSpec(
            num_scalar_prefetch=2,
            grid=(blocks,),
            in_specs=[
                pl.BlockSpec((QB, wide), by_block),
                whole(kt.shape),
                whole(v.shape),
                pl.BlockSpec((QB, 3), by_block),
                whole(kpos.shape),
                pl.BlockSpec((QB, 1), by_block),
                whole(kid.shape),
                whole(cen.shape),
                whole(amp.shape),
                whole(lnorm.shape),
                whole(wpt.shape),
            ],
            out_specs=[
                pl.BlockSpec((1, tiles, groups * rows, TILE), lambda b, *_: (b, 0, 0, 0)),
                pl.BlockSpec((QB, wide), by_block),
                pl.BlockSpec((groups * rows, TILE), by_block),
            ],
            scratch_shapes=[
                pltpu.VMEM((groups, rows, GW), bf16),
                pltpu.VMEM((tiles, groups * rows, TILE), f32),
                pltpu.VMEM((groups * rows, TILE), f32),
                pltpu.VMEM((QB, TILE), f32),
                pltpu.VMEM((QB, TILE), f32),
                pltpu.VMEM((kernels, QB * TILE), bf16),
                pltpu.VMEM((heads, QB * TILE), f32),
                pltpu.VMEM((groups, rows, GW), f32),
                pltpu.VMEM((groups * rows, TILE), f32),
            ],
        ),
        out_shape=[
            jax.ShapeDtypeStruct((blocks, tiles, groups * rows, TILE), bf16),
            jax.ShapeDtypeStruct(q.shape, f32),
            jax.ShapeDtypeStruct((blocks * groups * rows, TILE), f32),
        ],
        compiler_params=pltpu.CompilerParams(vmem_limit_bytes=60 << 20),
        name="attend",
    )(lo, hi, q, kt, v, qpos, kpos, qid, kid, cen, amp, lnorm, wpt)


def attention_backward(lo, hi, p, rl, q, do, o, k, vt, qpos, kpos, cen, amp, lnorm, wp, head_dim):
    tiles = vt.shape[0]
    wide = q.shape[1]
    groups = wide // GW
    rows = QB * HG
    blocks = q.shape[0] // QB
    kernels, heads = wp.shape
    by_block = lambda b, *_: (b, 0)
    return pl.pallas_call(
        functools.partial(bwd_kernel, head_dim),
        grid_spec=pltpu.PrefetchScalarGridSpec(
            num_scalar_prefetch=2,
            grid=(blocks,),
            in_specs=[
                pl.BlockSpec((1, tiles, groups * rows, TILE), lambda b, *_: (b, 0, 0, 0)),
                pl.BlockSpec((groups * rows, TILE), by_block),
                pl.BlockSpec((QB, wide), by_block),
                pl.BlockSpec((QB, wide), by_block),
                pl.BlockSpec((QB, wide), by_block),
                whole(k.shape),
                whole(vt.shape),
                pl.BlockSpec((QB, 3), by_block),
                whole(kpos.shape),
                whole(cen.shape),
                whole(amp.shape),
                whole(lnorm.shape),
                whole(wp.shape),
            ],
            out_specs=[
                pl.BlockSpec((QB, wide), by_block),
                whole(vt.shape),
                whole(vt.shape),
                whole((heads, kernels)),
                whole((3, kernels, TILE)),
            ],
            scratch_shapes=[
                pltpu.VMEM((groups, GW, rows), bf16),
                pltpu.VMEM((groups, rows, GW), bf16),
                pltpu.VMEM((groups, GW, rows), bf16),
                pltpu.VMEM((groups * rows, TILE), f32),
                pltpu.VMEM((groups, rows, GW), f32),
                pltpu.VMEM((heads, QB * TILE), bf16),
                pltpu.VMEM((QB, TILE), f32),
                pltpu.VMEM((kernels, QB * TILE), bf16),
                pltpu.VMEM((kernels, QB * TILE), f32),
            ],
        ),
        out_shape=[
            jax.ShapeDtypeStruct(q.shape, f32),
            jax.ShapeDtypeStruct(vt.shape, f32),
            jax.ShapeDtypeStruct(vt.shape, f32),
            jax.ShapeDtypeStruct((heads, kernels), f32),
            jax.ShapeDtypeStruct((3, kernels, TILE), f32),
        ],
        compiler_params=pltpu.CompilerParams(vmem_limit_bytes=60 << 20),
        name="attend_back",
    )(lo, hi, p, rl, q, do, o, k, vt, qpos, kpos, cen, amp, lnorm, wp)


def on_device(
    atoms,
    coords,
    atom_types,
    lengths,
    times,
    type_table,
    gain_one,
    shift_one,
    w_qkv,
    centers,
    widths,
    w_pair,
    w_out,
    gain_two,
    shift_two,
    w_up,
    w_down,
    w_force,
    out_grad,
    force_grad,
):
    micro_count, row_count, model_width = atoms.shape
    head_count = w_pair.shape[1]
    head_dim = model_width // head_count
    score_scale = head_dim ** (-0.5)
    my_index = lax.axis_index("row")
    my_core = lax.axis_index("wt")
    row_size = lax.axis_size("row")
    reach_shards = (MAXLEN - 2) // row_count + 1
    all_rows = row_count * row_size
    groups = head_count // HG
    used = HG * head_dim
    covers = row_size <= 2 * reach_shards + 1
    span = row_size if covers else 2 * reach_shards + 1
    key_count = span * row_count
    key_base = 0 if covers else (my_index - reach_shards) * row_count
    type_codes = jnp.arange(type_table.shape[0], dtype=jnp.int32)

    def fetch(x, axis):
        if covers:
            return lax.all_gather(x, "row", axis=axis, tiled=True)
        far = [shifted(x, "row", by) for by in range(reach_shards, 0, -1)]
        near = [shifted(x, "row", -by) for by in range(1, reach_shards + 1)]
        return jnp.concatenate(far + [x] + near, axis=axis)

    def send_back(x):
        if covers:
            return lax.psum_scatter(x.astype(bf16), "row", scatter_dimension=0, tiled=True).astype(f32)
        shards = x.reshape(span, row_count, model_width)
        own = shards[reach_shards]
        for offset in range(1, reach_shards + 1):
            for by in (offset, -offset):
                own = own + shifted(shards[reach_shards - by].astype(bf16), "row", -by).astype(f32)
        return own

    def padded(x, axis):
        split = x.reshape(x.shape[:axis] + (groups, used) + x.shape[axis + 1 :])
        pads = [(0, 0)] * split.ndim
        pads[axis + 1] = (0, GW - used)
        return jnp.pad(split, pads).reshape(x.shape[:axis] + (groups * GW,) + x.shape[axis + 1 :])

    def unpadded(x, axis):
        split = x.reshape(x.shape[:axis] + (groups, GW) + x.shape[axis + 1 :])
        split = lax.slice_in_dim(split, 0, used, axis=axis + 1)
        return split.reshape(x.shape[:axis] + (groups * used,) + x.shape[axis + 1 :])

    w_qkv_full = lax.all_gather(w_qkv, "wt", axis=0, tiled=True)
    w_out_full = lax.all_gather(w_out, "wt", axis=0, tiled=True)
    w_up_full = lax.all_gather(w_up, "wt", axis=0, tiled=True)
    w_down_full = lax.all_gather(w_down, "wt", axis=0, tiled=True)
    w_q = padded(w_qkv_full[:, :model_width], 1)
    w_k = padded(w_qkv_full[:, model_width : 2 * model_width], 1)
    w_v = padded(w_qkv_full[:, 2 * model_width :], 1)

    item_ends = jnp.cumsum(lengths[0])
    own_places = my_index * row_count + jnp.arange(row_count, dtype=jnp.int32)
    own_ids = item_ids(own_places, item_ends)
    key_places = key_base + jnp.arange(key_count, dtype=jnp.int32)
    inside = (key_places >= 0) & (key_places < all_rows)
    key_ids = jnp.where(inside, item_ids(key_places, item_ends), -1)
    first_places = own_places[::QB]
    last_places = own_places[QB - 1 :: QB]
    begins = jnp.max(jnp.where(item_ends[None, :] <= first_places[:, None], item_ends[None, :], 0), axis=1)
    ends = jnp.min(
        jnp.where(item_ends[None, :] > last_places[:, None], item_ends[None, :], all_rows), axis=1
    )
    tiles = key_count // TILE
    lo = jnp.clip((begins - key_base) // TILE, 0, tiles)
    hi = jnp.clip((ends - key_base + TILE - 1) // TILE, 0, tiles)

    onehot = (atom_types[0][:, None] == type_codes[None, :]).astype(bf16)
    base_rows = (
        atoms[0].astype(f32)
        + time_code(times[0], model_width)
        + jnp.dot(onehot, type_table, preferred_element_type=f32)
    )
    normed_one, inverse_one = norm_parts(base_rows)
    normed_in = (normed_one * gain_one + shift_one).astype(bf16)
    every = fetch(normed_in, 0)
    positions = fetch(coords[:, 0, :], 1).astype(f32)

    queries = jnp.dot(normed_in, w_q, preferred_element_type=f32).astype(bf16)
    keys = jnp.dot(every, w_k, preferred_element_type=f32).astype(bf16)
    values = jnp.dot(every, w_v, preferred_element_type=f32).astype(bf16)
    wide = groups * GW
    by_tile = lambda x: x.reshape(tiles, TILE, wide)
    keys, values = by_tile(keys), by_tile(values)
    keys_t = jnp.swapaxes(keys, 1, 2)
    values_t = jnp.swapaxes(values, 1, 2)
    qpos = jnp.transpose(coords[:, 0, :].astype(f32))
    kpos = jnp.swapaxes(positions.reshape(3, tiles, TILE), 0, 1)
    qid = own_ids[:, None]
    kid = key_ids.reshape(tiles, 1, TILE)
    steep = math.sqrt(0.5 * LOG2E)
    lanes = lambda x: jnp.broadcast_to(x[:, None], (x.shape[0], TILE))
    cen, amp = lanes(centers), lanes(steep / widths)
    lnorm = lanes(-jnp.log2(math.sqrt(2.0 * math.pi) * widths))

    probs, att_wide, inverse_total = attention_forward(
        lo, hi, queries, keys_t, values, qpos, kpos, qid, kid, cen, amp, lnorm,
        jnp.transpose(w_pair), head_dim,
    )
    attended = unpadded(att_wide, 1)
    att_low = attended.astype(bf16)
    after_att = base_rows + jnp.dot(att_low, w_out_full, preferred_element_type=f32)
    normed_two, inverse_two = norm_parts(after_att)
    ffn_in = (normed_two * gain_two + shift_two).astype(bf16)
    hidden = jnp.dot(ffn_in, w_up_full, preferred_element_type=f32)
    activated_full, gelu_pull = jax.vjp(gelu_tanh, hidden)
    activated = activated_full.astype(bf16)
    block_sum = after_att + jnp.dot(activated, w_down_full, preferred_element_type=f32)
    out_low = block_sum.astype(bf16)
    force_rows = along_rows(w_force, out_low)
    force_cot = force_grad[:, 0, :]
    grad_sum = out_grad[0].astype(f32) + lax.dot_general(
        force_cot,
        w_force.astype(f32),
        (((0,), (0,)), ((), ())),
        precision=HIGHEST,
        preferred_element_type=f32,
    )
    grad_force = jnp.dot(
        force_cot, out_low.astype(f32), precision=HIGHEST, preferred_element_type=f32
    )
    grad_sum_low = grad_sum.astype(bf16)
    grad_act_low = along_rows(grad_sum_low, w_down_full).astype(bf16)
    grad_hidden_low = gelu_pull(grad_act_low.astype(f32))[0].astype(bf16)
    grad_ffn_in = along_rows(grad_hidden_low, w_up_full)
    grad_norm_two, grad_gain_two, grad_shift_two = norm_back(
        grad_ffn_in, normed_two, inverse_two, gain_two
    )
    grad_after = grad_sum + grad_norm_two
    grad_after_low = grad_after.astype(bf16)
    grad_att_low = along_rows(grad_after_low, w_out_full).astype(bf16)

    def my_half(x):
        half = x.shape[1] // 2
        return jnp.where(my_core == 0, x[:, :half], x[:, half:])

    def other_half(x):
        half = x.shape[1] // 2
        return jnp.where(my_core == 0, x[:, half:], x[:, :half])

    def weight_grad(left, right):
        lefts = jnp.concatenate([my_half(left), swap_cores(other_half(left))], axis=0)
        rights = jnp.concatenate([right, swap_cores(right)], axis=0)
        return cross_rows(lefts, rights).astype(bf16)

    def over_rows(x):
        return lax.psum_scatter(x, "row", scatter_dimension=1, tiled=True).astype(f32)

    w_down_grad = over_rows(weight_grad(activated, grad_sum_low))
    w_up_grad = over_rows(weight_grad(ffn_in, grad_hidden_low))
    w_out_grad = over_rows(weight_grad(att_low, grad_after_low))

    dq, dkt, dvt, pair_t, kernel_sums = attention_backward(
        lo, hi, probs, inverse_total, queries, padded(grad_att_low, 1), att_wide, keys, values_t,
        qpos, kpos, cen, amp, lnorm, w_pair, head_dim,
    )
    query_grad = (dq * score_scale).astype(bf16)
    key_grad = (jnp.swapaxes(dkt, 1, 2).reshape(key_count, wide) * score_scale).astype(bf16)
    value_grad = jnp.swapaxes(dvt, 1, 2).reshape(key_count, wide).astype(bf16)
    grad_every = along_rows(key_grad, w_k) + along_rows(value_grad, w_v)
    grad_normed_in = along_rows(query_grad, w_q) + send_back(grad_every)
    qkv_grad_w = jnp.concatenate(
        [
            unpadded(cross_rows(normed_in, query_grad), 1),
            unpadded(cross_rows(every, key_grad), 1),
            unpadded(cross_rows(every, value_grad), 1),
        ],
        axis=1,
    ).astype(bf16)
    w_qkv_grad = over_rows(lax.psum_scatter(qkv_grad_w, "wt", scatter_dimension=0, tiled=True))
    grad_norm_one, grad_gain_one, grad_shift_one = norm_back(
        grad_normed_in, normed_one, inverse_one, gain_one
    )
    atoms_grad = grad_after + grad_norm_one
    grad_table = lax.dot_general(
        onehot.astype(f32),
        atoms_grad,
        (((0,), (0,)), ((), ())),
        precision=HIGHEST,
        preferred_element_type=f32,
    )
    sums = jnp.sum(kernel_sums, axis=2)
    center_part = sums[1] / (steep * widths)
    width_part = (sums[2] / (steep * steep) - sums[0]) / widths
    small_sums = lax.psum(
        (
            grad_table,
            grad_gain_one,
            grad_shift_one,
            center_part,
            width_part,
            jnp.transpose(pair_t),
            grad_gain_two,
            grad_shift_two,
            grad_force,
        ),
        ("row", "wt"),
    )
    return (
        out_low[None],
        force_rows[:, None, :],
        atoms_grad[None],
        small_sums[0],
        small_sums[1],
        small_sums[2],
        w_qkv_grad,
        small_sums[3],
        small_sums[4],
        small_sums[5],
        w_out_grad,
        small_sums[6],
        small_sums[7],
        w_up_grad,
        w_down_grad,
        small_sums[8],
    )


def solution(mesh):
    in_specs = (
        P("wt", "row", None),
        P(None, "wt", "row"),
        P("wt", "row"),
        P("wt", None),
        P("wt"),
        P(),
        P(),
        P(),
        P("wt", None),
        P(),
        P(),
        P(),
        P("wt", None),
        P(),
        P(),
        P("wt", None),
        P("wt", None),
        P(),
        P("wt", "row", None),
        P(None, "wt", "row"),
    )
    out_specs = (
        P("wt", "row", None),
        P(None, "wt", "row"),
        P("wt", "row", None),
        P(),
        P(),
        P(),
        P("wt", "row"),
        P(),
        P(),
        P(),
        P("wt", "row"),
        P(),
        P(),
        P("wt", "row"),
        P("wt", "row"),
        P(),
    )
    return jax.shard_map(
        on_device, mesh=mesh, in_specs=in_specs, out_specs=out_specs, check_vma=False
    )
```

```python
import functools
import math

import jax
import jax.numpy as jnp
from jax import lax
from jax.experimental import pallas as pl
from jax.experimental.pallas import tpu as pltpu
from jax.sharding import PartitionSpec as P

MAXLEN = 1024
NEG_FILL = -1e30
HIGHEST = lax.Precision.HIGHEST
QB = 32
TILE = 128
HG = 8
GW = 256
LOG2E = 1.4426950408889634
bf16 = jnp.bfloat16
f32 = jnp.float32


def shifted(x, axis, by):
    length = lax.axis_size(axis)
    pairs = [(i, i + by) for i in range(length) if 0 <= i + by < length]
    return lax.ppermute(x, axis, pairs)


def swap_cores(x):
    return lax.ppermute(x, "wt", [(0, 1), (1, 0)])


def norm_parts(values_in):
    average = jnp.mean(values_in, axis=-1, keepdims=True)
    centred = values_in - average
    inverse = lax.rsqrt(jnp.mean(centred * centred, axis=-1, keepdims=True) + 1e-05)
    return (centred * inverse, inverse)


def norm_back(grad_out, normed, inverse, gain_vec):
    grad_normed = grad_out * gain_vec
    mean_grad = jnp.mean(grad_normed, axis=-1, keepdims=True)
    mean_mixed = jnp.mean(grad_normed * normed, axis=-1, keepdims=True)
    grad_in = inverse * (grad_normed - mean_grad - normed * mean_mixed)
    return (grad_in, jnp.sum(grad_out * normed, axis=0), jnp.sum(grad_out, axis=0))


def gelu_tanh(values_in):
    return (
        0.5
        * values_in
        * (
            1.0
            + jnp.tanh(
                0.7978845608028654 * (values_in + 0.044715 * values_in * values_in * values_in)
            )
        )
    )


def time_code(moment, model_width):
    half_width = model_width // 2
    frequency = jnp.exp(-math.log(10000.0) * jnp.arange(half_width, dtype=jnp.float32) / half_width)
    angles = 100.0 * moment * frequency
    return jnp.concatenate([jnp.sin(angles), jnp.cos(angles)])


def item_ids(places, item_ends):
    return jnp.sum((places[:, None] >= item_ends[None, :]).astype(jnp.int32), axis=1)


def cross_rows(left_side, right_side):
    return lax.dot_general(
        left_side, right_side, (((0,), (0,)), ((), ())), preferred_element_type=jnp.float32
    )


def along_rows(left_side, right_side):
    return lax.dot_general(
        left_side, right_side, (((1,), (1,)), ((), ())), preferred_element_type=jnp.float32
    )


def head_mask(groups_dim):
    h = lax.broadcasted_iota(jnp.int32, (HG, GW), 0)
    f = lax.broadcasted_iota(jnp.int32, (HG, GW), 1)
    lo = h * groups_dim
    return (f >= lo) & (f < lo + groups_dim)


def expand(rows, mask):
    parts = [
        jnp.where(mask, jnp.broadcast_to(rows[i : i + 1, :], (HG, GW)), 0.0)
        for i in range(rows.shape[0])
    ]
    return jnp.concatenate(parts, axis=0)


def collapse(stacked, mask):
    count = stacked.shape[0] // HG
    parts = [
        jnp.sum(jnp.where(mask, stacked[i * HG : (i + 1) * HG, :], 0.0), axis=0, keepdims=True)
        for i in range(count)
    ]
    return jnp.concatenate(parts, axis=0)


def tile_distance(qpos_ref, kpos_ref, tile):
    total = None
    for axis in range(3):
        differ = qpos_ref[:, axis : axis + 1] - kpos_ref[tile, axis : axis + 1, :]
        total = differ * differ if total is None else total + differ * differ
    return jnp.sqrt(total)


def fwd_kernel(
    head_dim, lo_ref, hi_ref, q_ref, kt_ref, v_ref, qpos_ref, kpos_ref, qid_ref, kid_ref,
    cen_ref, amp_ref, lnorm_ref, wpt_ref, p_ref, o_ref, rl_ref,
    qexp, score, top, dist, neg, kern, bias, acc, total,
):
    block = pl.program_id(0)
    lo, hi = lo_ref[block], hi_ref[block]
    groups = wpt_ref.shape[0] // HG
    rows = QB * HG
    scale = head_dim ** (-0.5)
    mask = head_mask(head_dim)
    for g in range(groups):
        qexp[g] = expand(q_ref[:, g * GW : (g + 1) * GW].astype(f32), mask).astype(bf16)
        acc[g] = jnp.zeros((rows, GW), f32)
    top[...] = jnp.full(top.shape, NEG_FILL, f32)
    total[...] = jnp.zeros(total.shape, f32)

    def first(tile, carry):
        dist[...] = tile_distance(qpos_ref, kpos_ref, tile)
        neg[...] = jnp.where(qid_ref[:, 0:1] == kid_ref[tile], 0.0, NEG_FILL)

        def some_kernels(cg, carry):
            at = pl.ds(pl.multiple_of(cg * 16, 16), 16)
            cen, amp, lnorm = cen_ref[at, :], amp_ref[at, :], lnorm_ref[at, :]
            for i in range(QB):
                t = (dist[i : i + 1, :] - cen) * amp
                kern[at, i * TILE : (i + 1) * TILE] = jnp.exp2(lnorm - t * t).astype(bf16)
            return carry

        lax.fori_loop(0, cen_ref.shape[0] // 16, some_kernels, 0)
        for part in range(QB // 8):
            at = slice(part * 8 * TILE, (part + 1) * 8 * TILE)
            bias[:, at] = jnp.dot(wpt_ref[...], kern[:, at], preferred_element_type=f32)
        for g in range(groups):
            dots = jnp.dot(qexp[g], kt_ref[tile, g * GW : (g + 1) * GW, :], preferred_element_type=f32)
            for i in range(QB):
                here = slice(g * rows + i * HG, g * rows + (i + 1) * HG)
                value = (
                    dots[i * HG : (i + 1) * HG, :] * scale
                    + bias[g * HG : (g + 1) * HG, i * TILE : (i + 1) * TILE]
                    + neg[i : i + 1, :]
                )
                score[tile, here, :] = value
                top[here, :] = jnp.maximum(top[here, :], value)
        return carry

    lax.fori_loop(lo, hi, first, 0)
    top[...] = jnp.broadcast_to(jnp.max(top[...], axis=1, keepdims=True), top.shape)

    def second(tile, carry):
        for g in range(groups):
            here = slice(g * rows, (g + 1) * rows)
            prob = jnp.exp(score[tile, here, :] - top[here, :])
            total[here, :] += prob
            low = prob.astype(bf16)
            p_ref[0, tile, here, :] = low
            acc[g] += jnp.dot(low, v_ref[tile, :, g * GW : (g + 1) * GW], preferred_element_type=f32)
        return carry

    lax.fori_loop(lo, hi, second, 0)
    for g in range(groups):
        here = slice(g * rows, (g + 1) * rows)
        inverse = 1.0 / jnp.sum(total[here, :], axis=1, keepdims=True)
        rl_ref[here, :] = jnp.broadcast_to(inverse, (rows, TILE))
        o_ref[:, g * GW : (g + 1) * GW] = collapse(acc[g] * inverse, mask)


def bwd_kernel(
    head_dim, lo_ref, hi_ref, p_ref, rl_ref, q_ref, do_ref, o_ref, k_ref, vt_ref, qpos_ref, kpos_ref,
    cen_ref, amp_ref, lnorm_ref, wp_ref, dq_ref, dkt_ref, dvt_ref, m0_ref, sums_ref,
    qext, doexp, doext, delta, dqacc, glow, dist, kern, gk, dkt_acc, dvt_acc,
):
    block = pl.program_id(0)
    lo, hi = lo_ref[block], hi_ref[block]
    groups = q_ref.shape[1] // GW
    rows = QB * HG
    scale = head_dim ** (-0.5)
    mask = head_mask(head_dim)

    @pl.when(block == 0)
    def _():
        dkt_acc[...] = jnp.zeros(dkt_acc.shape, f32)
        dvt_acc[...] = jnp.zeros(dvt_acc.shape, f32)
        m0_ref[...] = jnp.zeros(m0_ref.shape, f32)
        sums_ref[...] = jnp.zeros(sums_ref.shape, f32)

    for g in range(groups):
        lanes = slice(g * GW, (g + 1) * GW)
        here = slice(g * rows, (g + 1) * rows)
        inverse = rl_ref[here, 0:1]
        qext[g] = jnp.transpose(expand(q_ref[:, lanes].astype(f32), mask)).astype(bf16)
        grads = do_ref[:, lanes].astype(f32)
        both = expand(grads, mask) * inverse
        doexp[g] = both.astype(bf16)
        doext[g] = jnp.transpose(both).astype(bf16)
        mixed = jnp.sum(expand(grads * o_ref[:, lanes], mask), axis=1, keepdims=True) * inverse
        delta[here, :] = jnp.broadcast_to(mixed, (rows, TILE))
        dqacc[g] = jnp.zeros((rows, GW), f32)

    def one_tile(tile, carry):
        keys = pl.ds(pl.multiple_of(tile * TILE, TILE), TILE)
        dist[...] = tile_distance(qpos_ref, kpos_ref, tile)
        for pair in range(groups // 2):
            grads = []
            for g in (2 * pair, 2 * pair + 1):
                lanes = slice(g * GW, (g + 1) * GW)
                here = slice(g * rows, (g + 1) * rows)
                low = p_ref[0, tile, here, :]
                dp = jnp.dot(doexp[g], vt_ref[tile, lanes, :], preferred_element_type=f32)
                gl = low.astype(f32) * (dp - delta[here, :])
                grads.append(gl)
                gl_low = gl.astype(bf16)
                dqacc[g] += jnp.dot(gl_low, k_ref[tile, :, lanes], preferred_element_type=f32)
                dkt_acc[lanes, keys] += jnp.dot(qext[g], gl_low, preferred_element_type=f32)
                dvt_acc[lanes, keys] += jnp.dot(doext[g], low, preferred_element_type=f32)
            for i in range(QB):
                at = slice(i * HG, (i + 1) * HG)
                glow[pair * 16 : (pair + 1) * 16, i * TILE : (i + 1) * TILE] = jnp.concatenate(
                    [grads[0][at, :], grads[1][at, :]], axis=0
                ).astype(bf16)
        for part in range(QB // 8):
            at = slice(part * 8 * TILE, (part + 1) * 8 * TILE)
            gk[:, at] = jnp.dot(wp_ref[...], glow[:, at], preferred_element_type=f32)

        def some_kernels(cg, carry):
            at = pl.ds(pl.multiple_of(cg * 16, 16), 16)
            cen, amp, lnorm = cen_ref[at, :], amp_ref[at, :], lnorm_ref[at, :]
            plain = jnp.zeros((16, TILE), f32)
            once = jnp.zeros((16, TILE), f32)
            twice = jnp.zeros((16, TILE), f32)
            for i in range(QB):
                lanes = slice(i * TILE, (i + 1) * TILE)
                t = (dist[i : i + 1, :] - cen) * amp
                value = jnp.exp2(lnorm - t * t)
                kern[at, lanes] = value.astype(bf16)
                weighted = gk[at, lanes] * value
                plain = plain + weighted
                weighted = weighted * t
                once = once + weighted
                twice = twice + weighted * t
            sums_ref[0, at, :] += plain
            sums_ref[1, at, :] += once
            sums_ref[2, at, :] += twice
            return carry

        lax.fori_loop(0, cen_ref.shape[0] // 16, some_kernels, 0)
        m0_ref[...] += lax.dot_general(
            glow[...], kern[...], (((1,), (1,)), ((), ())), preferred_element_type=f32
        )
        return carry

    lax.fori_loop(lo, hi, one_tile, 0)
    for g in range(groups):
        dq_ref[:, g * GW : (g + 1) * GW] = (collapse(dqacc[g], mask) * scale).astype(bf16)

    @pl.when(block == pl.num_programs(0) - 1)
    def _():
        dkt_ref[...] = (dkt_acc[...] * scale).astype(bf16)
        dvt_ref[...] = dvt_acc[...].astype(bf16)


def whole(shape):
    return pl.BlockSpec(shape, lambda *_: (0,) * len(shape), pipeline_mode=pl.Buffered(1))


def attention_forward(lo, hi, q, kt, v, qpos, kpos, qid, kid, cen, amp, lnorm, wpt, head_dim):
    tiles = kt.shape[0]
    wide = q.shape[1]
    groups = wide // GW
    rows = QB * HG
    blocks = q.shape[0] // QB
    kernels, heads = cen.shape[0], wpt.shape[0]
    by_block = lambda b, *_: (b, 0)
    return pl.pallas_call(
        functools.partial(fwd_kernel, head_dim),
        grid_spec=pltpu.PrefetchScalarGridSpec(
            num_scalar_prefetch=2,
            grid=(blocks,),
            in_specs=[
                pl.BlockSpec((QB, wide), by_block),
                whole(kt.shape),
                whole(v.shape),
                pl.BlockSpec((QB, 3), by_block),
                whole(kpos.shape),
                pl.BlockSpec((QB, 1), by_block),
                whole(kid.shape),
                whole(cen.shape),
                whole(amp.shape),
                whole(lnorm.shape),
                whole(wpt.shape),
            ],
            out_specs=[
                pl.BlockSpec((1, tiles, groups * rows, TILE), lambda b, *_: (b, 0, 0, 0)),
                pl.BlockSpec((QB, wide), by_block),
                pl.BlockSpec((groups * rows, TILE), by_block),
            ],
            scratch_shapes=[
                pltpu.VMEM((groups, rows, GW), bf16),
                pltpu.VMEM((tiles, groups * rows, TILE), f32),
                pltpu.VMEM((groups * rows, TILE), f32),
                pltpu.VMEM((QB, TILE), f32),
                pltpu.VMEM((QB, TILE), f32),
                pltpu.VMEM((kernels, QB * TILE), bf16),
                pltpu.VMEM((heads, QB * TILE), f32),
                pltpu.VMEM((groups, rows, GW), f32),
                pltpu.VMEM((groups * rows, TILE), f32),
            ],
        ),
        out_shape=[
            jax.ShapeDtypeStruct((blocks, tiles, groups * rows, TILE), bf16),
            jax.ShapeDtypeStruct(q.shape, f32),
            jax.ShapeDtypeStruct((blocks * groups * rows, TILE), f32),
        ],
        compiler_params=pltpu.CompilerParams(vmem_limit_bytes=60 << 20),
        cost_estimate=pl.CostEstimate(
            flops=30_000_000_000, bytes_accessed=40_000_000, transcendentals=200_000_000
        ),
        name="attend",
    )(lo, hi, q, kt, v, qpos, kpos, qid, kid, cen, amp, lnorm, wpt)


def attention_backward(lo, hi, p, rl, q, do, o, k, vt, qpos, kpos, cen, amp, lnorm, wp, head_dim):
    tiles = vt.shape[0]
    wide = q.shape[1]
    groups = wide // GW
    rows = QB * HG
    blocks = q.shape[0] // QB
    kernels, heads = wp.shape
    by_block = lambda b, *_: (b, 0)
    return pl.pallas_call(
        functools.partial(bwd_kernel, head_dim),
        grid_spec=pltpu.PrefetchScalarGridSpec(
            num_scalar_prefetch=2,
            grid=(blocks,),
            in_specs=[
                pl.BlockSpec((1, tiles, groups * rows, TILE), lambda b, *_: (b, 0, 0, 0)),
                pl.BlockSpec((groups * rows, TILE), by_block),
                pl.BlockSpec((QB, wide), by_block),
                pl.BlockSpec((QB, wide), by_block),
                pl.BlockSpec((QB, wide), by_block),
                whole(k.shape),
                whole(vt.shape),
                pl.BlockSpec((QB, 3), by_block),
                whole(kpos.shape),
                whole(cen.shape),
                whole(amp.shape),
                whole(lnorm.shape),
                whole(wp.shape),
            ],
            out_specs=[
                pl.BlockSpec((QB, wide), by_block),
                whole((wide, tiles * TILE)),
                whole((wide, tiles * TILE)),
                whole((heads, kernels)),
                whole((3, kernels, TILE)),
            ],
            scratch_shapes=[
                pltpu.VMEM((groups, GW, rows), bf16),
                pltpu.VMEM((groups, rows, GW), bf16),
                pltpu.VMEM((groups, GW, rows), bf16),
                pltpu.VMEM((groups * rows, TILE), f32),
                pltpu.VMEM((groups, rows, GW), f32),
                pltpu.VMEM((heads, QB * TILE), bf16),
                pltpu.VMEM((QB, TILE), f32),
                pltpu.VMEM((kernels, QB * TILE), bf16),
                pltpu.VMEM((kernels, QB * TILE), f32),
                pltpu.VMEM((wide, tiles * TILE), f32),
                pltpu.VMEM((wide, tiles * TILE), f32),
            ],
        ),
        out_shape=[
            jax.ShapeDtypeStruct(q.shape, bf16),
            jax.ShapeDtypeStruct((wide, tiles * TILE), bf16),
            jax.ShapeDtypeStruct((wide, tiles * TILE), bf16),
            jax.ShapeDtypeStruct((heads, kernels), f32),
            jax.ShapeDtypeStruct((3, kernels, TILE), f32),
        ],
        compiler_params=pltpu.CompilerParams(vmem_limit_bytes=62 << 20),
        cost_estimate=pl.CostEstimate(
            flops=60_000_000_000, bytes_accessed=60_000_000, transcendentals=200_000_000
        ),
        name="attend_back",
    )(lo, hi, p, rl, q, do, o, k, vt, qpos, kpos, cen, amp, lnorm, wp)


MESH = pl.DeviceIdType.MESH
INNER = 4


def places():
    row, core = lax.axis_index("row"), lax.axis_index("wt")
    outer, inner = row // INNER, row % INNER
    return row, core, outer, inner


def plane_mates(inner):
    y, x = inner // 2, inner % 2
    return (y * 2 + (1 - x), (1 - y) * 2 + x, (1 - y) * 2 + (1 - x))


def greet(targets):
    barrier = pltpu.get_barrier_semaphore()
    for target in targets:
        pl.semaphore_signal(barrier, inc=1, device_id=target, device_id_type=MESH)
    pl.semaphore_wait(barrier, len(targets))


def remote(src, dst, send_sem, recv_sem, target):
    return pltpu.make_async_remote_copy(
        src_ref=src, dst_ref=dst, send_sem=send_sem, recv_sem=recv_sem,
        device_id=target, device_id_type=MESH,
    )


def gather_kernel(outers, x_ref, c_ref, xo_ref, co_ref, sends, gets, sends_c, gets_c):
    row, core, outer, inner = places()
    mates = plane_mates(inner)
    far = [(outer + step) % outers for step in range(1, outers)]
    plane = [(outer * INNER + mate, core) for mate in mates]
    column = [(other * INNER + inner, core) for other in far]
    greet(plane + column)
    started = []

    def send(src, src_c, slot, target):
        at = len(started) // 2
        for copy in (
            remote(src, xo_ref.at[slot], sends.at[at], gets.at[slot], target),
            remote(src_c, co_ref.at[slot], sends_c.at[at], gets_c.at[slot], target),
        ):
            copy.start()
            started.append(copy)

    for target in column:
        send(x_ref, c_ref, row, target)
    for target in plane:
        send(x_ref, c_ref, row, target)
    xo_ref[row] = x_ref[...]
    co_ref[row] = c_ref[...]

    def arrived(slot):
        remote(x_ref, xo_ref.at[slot], sends.at[0], gets.at[slot], (row, core)).wait_recv()
        remote(c_ref, co_ref.at[slot], sends_c.at[0], gets_c.at[slot], (row, core)).wait_recv()

    for step in range(1, outers):
        slot = ((outer + outers - step) % outers) * INNER + inner
        arrived(slot)
        for target in plane:
            send(xo_ref.at[slot], co_ref.at[slot], slot, target)
    for mate in mates:
        for step in range(outers):
            arrived(((outer + outers - step) % outers) * INNER + mate)
    for copy in started:
        copy.wait_send()


def gather_rows(x, c, rows):
    outers = rows // INNER
    count = (outers - 1) + 3 * outers
    vmem = pl.BlockSpec(memory_space=pltpu.VMEM)
    return pl.pallas_call(
        functools.partial(gather_kernel, outers),
        out_shape=[
            jax.ShapeDtypeStruct((rows,) + x.shape, x.dtype),
            jax.ShapeDtypeStruct((rows,) + c.shape, c.dtype),
        ],
        in_specs=[vmem, vmem],
        out_specs=[vmem, vmem],
        scratch_shapes=[
            pltpu.SemaphoreType.DMA((count,)),
            pltpu.SemaphoreType.DMA((rows,)),
            pltpu.SemaphoreType.DMA((count,)),
            pltpu.SemaphoreType.DMA((rows,)),
        ],
        compiler_params=pltpu.CompilerParams(
            collective_id=0, has_side_effects=True, vmem_limit_bytes=40 << 20
        ),
        name="gather_rows",
    )(x, c)


def finish_kernel(outers, part_width, dkt_ref, dvt_ref, dq_ref, every_ref, own_ref, wq_ref, wk_ref, wv_ref, xo_ref, wo_ref,
                  xs, xa, xm, xb, wp, wi, wa, wm, wb, w0_sems, a_send, a_recv, b_send, b_recv):
    row, core, outer, inner = places()
    mates = plane_mates(inner)
    count, width = own_ref.shape
    half = width // 2
    used = part_width * 8
    rows_each = wo_ref.shape[0]
    plane = [(outer * INNER + mate, core) for mate in mates]
    far = [(outer + step) % outers for step in range(1, outers)]
    column = [(other * INNER + inner, core) for other in far]
    order = far + [outer]
    greet(plane + column + [(row, 1 - core)])
    started = []

    def grad_chunk(slot):
        at = pl.ds(pl.multiple_of(slot * count, count), count)
        flipped = jnp.dot(wk_ref[...], dkt_ref[:, at], preferred_element_type=f32)
        flipped += jnp.dot(wv_ref[...], dvt_ref[:, at], preferred_element_type=f32)
        return jnp.transpose(flipped)

    def begin(copy):
        copy.start()
        started.append(copy)

    def to_mate(which, at, o, p, src, dst):
        return remote(src, dst, a_send.at[which, p, at], a_recv.at[which, p, o], plane[p])

    for at, o in enumerate(order):
        for p in range(3):
            xs[o, mates[p]] = grad_chunk(o * INNER + mates[p]).astype(bf16)
            begin(to_mate(0, at, o, p, xs.at[o, mates[p]], xa.at[p, o]))
    for o in order:
        xs[o, inner] = grad_chunk(o * INNER + inner).astype(bf16)

    def key_part(index, carry):
        g = index
        here = pl.ds(pl.multiple_of(g * GW, GW), used)
        there = pl.ds(pl.multiple_of(g * used, 16), used)
        wp[there, :] = lax.dot_general(
            dq_ref[:, pl.ds(pl.multiple_of(g * GW, GW), GW)], own_ref[...], (((0,), (0,)), ((), ())),
            preferred_element_type=f32,
        )[:used, :].astype(bf16)
        there = pl.ds(pl.multiple_of(width + g * used, 16), used)
        wp[there, :] = jnp.dot(dkt_ref[here, :], every_ref[...], preferred_element_type=f32).astype(bf16)
        there = pl.ds(pl.multiple_of(2 * width + g * used, 16), used)
        wp[there, :] = jnp.dot(dvt_ref[here, :], every_ref[...], preferred_element_type=f32).astype(bf16)
        return carry

    lax.fori_loop(0, width // used, key_part, 0)
    other_lanes = pl.ds(pl.multiple_of((1 - core) * half, 128), half)
    own_lanes = pl.ds(pl.multiple_of(core * half, 128), half)
    halves = remote(wp.at[:, other_lanes], wi, w0_sems.at[0], w0_sems.at[1], (row, 1 - core))
    halves.start()

    def plane_sum(which, own, got, o):
        total = own.astype(f32)
        for p in range(3):
            to_mate(which, 0, o, p, got.at[p, o], got.at[p, o]).wait_recv()
            total = total + got[p, o].astype(f32)
        return total

    def to_far(which, step, stage, last):
        return remote(
            stage.at[step], last.at[step], b_send.at[which, step], b_recv.at[which, step], column[step]
        )

    for step, o in enumerate(far):
        xm[step] = plane_sum(0, xs[o, inner], xa, o).astype(bf16)
        begin(to_far(0, step, xm, xb))
    halves.wait_recv()
    wi[...] = (wp[:, own_lanes].astype(f32) + wi[...].astype(f32)).astype(bf16)

    def w_rows(slot):
        return pl.ds(pl.multiple_of(slot * rows_each, 16), rows_each)

    for at, o in enumerate(order):
        for p in range(3):
            begin(to_mate(1, at, o, p, wi.at[w_rows(o * INNER + mates[p])], wa.at[p, o]))
    flipped = lax.dot_general(
        wq_ref[...], dq_ref[...], (((1,), (1,)), ((), ())), preferred_element_type=f32
    )
    total = plane_sum(0, xs[outer, inner], xa, outer) + jnp.transpose(flipped)
    for step in range(outers - 1):
        to_far(0, step, xm, xb).wait_recv()
        total = total + xb[step].astype(f32)
    xo_ref[...] = total
    for step, o in enumerate(far):
        wm[step] = plane_sum(1, wi[w_rows(o * INNER + inner), :], wa, o).astype(bf16)
        begin(to_far(1, step, wm, wb))
    total = plane_sum(1, wi[w_rows(outer * INNER + inner), :], wa, outer)
    for step in range(outers - 1):
        to_far(1, step, wm, wb).wait_recv()
        total = total + wb[step].astype(f32)
    wo_ref[...] = total
    halves.wait_send()
    for copy in started:
        copy.wait_send()


def finish_rows(dkt, dvt, dq, every, own, w_q, w_k, w_v, rows, head_dim):
    outers = rows // INNER
    count, width = own.shape
    each = 3 * width // rows
    half = width // 2
    vmem = pl.BlockSpec(memory_space=pltpu.VMEM)
    return pl.pallas_call(
        functools.partial(finish_kernel, outers, head_dim),
        out_shape=[
            jax.ShapeDtypeStruct((count, width), f32),
            jax.ShapeDtypeStruct((each, half), f32),
        ],
        in_specs=[vmem] * 8,
        out_specs=[vmem] * 2,
        scratch_shapes=[
            pltpu.VMEM((outers, INNER, count, width), bf16),
            pltpu.VMEM((3, outers, count, width), bf16),
            pltpu.VMEM((outers - 1, count, width), bf16),
            pltpu.VMEM((outers - 1, count, width), bf16),
            pltpu.VMEM((3 * width, width), bf16),
            pltpu.VMEM((3 * width, half), bf16),
            pltpu.VMEM((3, outers, each, half), bf16),
            pltpu.VMEM((outers - 1, each, half), bf16),
            pltpu.VMEM((outers - 1, each, half), bf16),
            pltpu.SemaphoreType.DMA((2,)),
            pltpu.SemaphoreType.DMA((2, 3, outers)),
            pltpu.SemaphoreType.DMA((2, 3, outers)),
            pltpu.SemaphoreType.DMA((2, outers - 1)),
            pltpu.SemaphoreType.DMA((2, outers - 1)),
        ],
        compiler_params=pltpu.CompilerParams(
            collective_id=1, has_side_effects=True, vmem_limit_bytes=60 << 20
        ),
        name="finish_rows",
    )(dkt, dvt, dq, every, own, w_q, w_k, w_v)


def total_kernel(count, x_ref, out_ref, got, s1, r1, s2, r2):
    row, core = lax.axis_index("row"), lax.axis_index("wt")
    me = row * 2 + core
    barrier = pltpu.get_barrier_semaphore()

    def place(step):
        other = (me + step) % count
        return other, (other // 2, other % 2)

    def hello(step, carry):
        pl.semaphore_signal(barrier, inc=1, device_id=place(step)[1], device_id_type=MESH)
        return carry

    lax.fori_loop(1, count, hello, 0)
    pl.semaphore_wait(barrier, count - 1)

    def first(step):
        other, target = place(step)
        return remote(x_ref.at[other], got.at[step], s1.at[step], r1.at[step], target)

    def second(step):
        return remote(out_ref.at[me], out_ref.at[me], s2.at[step], r2.at[step], place(step)[1])

    def from_other(step):
        other = (me + count - step) % count
        return remote(out_ref.at[me], out_ref.at[other], s2.at[step], r2.at[step], place(step)[1])

    def start_first(step, carry):
        first(step).start()
        return carry

    def add(step, total):
        first(step).wait_recv()
        return total + got[step]

    def start_second(step, carry):
        second(step).start()
        return carry

    def end(step, carry):
        from_other(step).wait_recv()
        first(step).wait_send()
        second(step).wait_send()
        return carry

    lax.fori_loop(1, count, start_first, 0)
    out_ref[me] = lax.fori_loop(1, count, add, x_ref[me])
    lax.fori_loop(1, count, start_second, 0)
    lax.fori_loop(1, count, end, 0)


def total_over_all(x):
    count = x.shape[0]
    vmem = pl.BlockSpec(memory_space=pltpu.VMEM)
    return pl.pallas_call(
        functools.partial(total_kernel, count),
        out_shape=jax.ShapeDtypeStruct(x.shape, f32),
        in_specs=[vmem],
        out_specs=vmem,
        scratch_shapes=[pltpu.VMEM(x.shape, f32)] + [pltpu.SemaphoreType.DMA((count,))] * 4,
        compiler_params=pltpu.CompilerParams(collective_id=2, has_side_effects=True),
        name="total_over_all",
    )(x)


def on_device(
    atoms,
    coords,
    atom_types,
    lengths,
    times,
    type_table,
    gain_one,
    shift_one,
    w_qkv,
    centers,
    widths,
    w_pair,
    w_out,
    gain_two,
    shift_two,
    w_up,
    w_down,
    w_force,
    out_grad,
    force_grad,
):
    micro_count, row_count, model_width = atoms.shape
    head_count = w_pair.shape[1]
    head_dim = model_width // head_count
    score_scale = head_dim ** (-0.5)
    my_index = lax.axis_index("row")
    my_core = lax.axis_index("wt")
    row_size = lax.axis_size("row")
    reach_shards = (MAXLEN - 2) // row_count + 1
    all_rows = row_count * row_size
    groups = head_count // HG
    used = HG * head_dim
    covers = row_size <= 2 * reach_shards + 1
    span = row_size if covers else 2 * reach_shards + 1
    key_count = span * row_count
    key_base = 0 if covers else (my_index - reach_shards) * row_count
    type_codes = jnp.arange(type_table.shape[0], dtype=jnp.int32)

    def fetch(x, axis):
        if covers:
            return lax.all_gather(x, "row", axis=axis, tiled=True)
        far = [shifted(x, "row", by) for by in range(reach_shards, 0, -1)]
        near = [shifted(x, "row", -by) for by in range(1, reach_shards + 1)]
        return jnp.concatenate(far + [x] + near, axis=axis)

    def send_back(x):
        if covers:
            return lax.psum_scatter(x.astype(bf16), "row", scatter_dimension=0, tiled=True).astype(f32)
        shards = x.reshape(span, row_count, model_width)
        own = shards[reach_shards]
        for offset in range(1, reach_shards + 1):
            for by in (offset, -offset):
                own = own + shifted(shards[reach_shards - by].astype(bf16), "row", -by).astype(f32)
        return own

    def padded(x, axis):
        split = x.reshape(x.shape[:axis] + (groups, used) + x.shape[axis + 1 :])
        pads = [(0, 0)] * split.ndim
        pads[axis + 1] = (0, GW - used)
        return jnp.pad(split, pads).reshape(x.shape[:axis] + (groups * GW,) + x.shape[axis + 1 :])

    def unpadded(x, axis):
        split = x.reshape(x.shape[:axis] + (groups, GW) + x.shape[axis + 1 :])
        split = lax.slice_in_dim(split, 0, used, axis=axis + 1)
        return split.reshape(x.shape[:axis] + (groups * used,) + x.shape[axis + 1 :])

    w_qkv_full = lax.all_gather(w_qkv, "wt", axis=0, tiled=True)
    w_out_full = lax.all_gather(w_out, "wt", axis=0, tiled=True)
    w_up_full = lax.all_gather(w_up, "wt", axis=0, tiled=True)
    w_down_full = lax.all_gather(w_down, "wt", axis=0, tiled=True)
    w_q = padded(w_qkv_full[:, :model_width], 1)
    w_k = padded(w_qkv_full[:, model_width : 2 * model_width], 1)
    w_v = padded(w_qkv_full[:, 2 * model_width :], 1)

    item_ends = jnp.cumsum(lengths[0])
    own_places = my_index * row_count + jnp.arange(row_count, dtype=jnp.int32)
    own_ids = item_ids(own_places, item_ends)
    key_places = key_base + jnp.arange(key_count, dtype=jnp.int32)
    inside = (key_places >= 0) & (key_places < all_rows)
    key_ids = jnp.where(inside, item_ids(key_places, item_ends), -1)
    first_places = own_places[::QB]
    last_places = own_places[QB - 1 :: QB]
    begins = jnp.max(jnp.where(item_ends[None, :] <= first_places[:, None], item_ends[None, :], 0), axis=1)
    ends = jnp.min(
        jnp.where(item_ends[None, :] > last_places[:, None], item_ends[None, :], all_rows), axis=1
    )
    tiles = key_count // TILE
    lo = jnp.clip((begins - key_base) // TILE, 0, tiles)
    hi = jnp.clip((ends - key_base + TILE - 1) // TILE, 0, tiles)

    onehot = (atom_types[0][:, None] == type_codes[None, :]).astype(bf16)
    base_rows = (
        atoms[0].astype(f32)
        + time_code(times[0], model_width)
        + jnp.dot(onehot, type_table, preferred_element_type=f32)
    )
    normed_one, inverse_one = norm_parts(base_rows)
    normed_in = (normed_one * gain_one + shift_one).astype(bf16)
    if covers:
        low_pos = jnp.pad(coords[:, 0, :], ((0, 13), (0, 0)))
        every, every_pos = gather_rows(normed_in, low_pos, row_size)
        every = every.reshape(key_count, model_width)
        kpos = every_pos[:, :3, :].astype(f32)
    else:
        every = fetch(normed_in, 0)
        positions = fetch(coords[:, 0, :], 1).astype(f32)
        kpos = jnp.swapaxes(positions.reshape(3, tiles, TILE), 0, 1)

    queries = jnp.dot(normed_in, w_q, preferred_element_type=f32).astype(bf16)
    keys = jnp.dot(every, w_k, preferred_element_type=f32).astype(bf16)
    values = jnp.dot(every, w_v, preferred_element_type=f32).astype(bf16)
    wide = groups * GW
    by_tile = lambda x: x.reshape(tiles, TILE, wide)
    keys, values = by_tile(keys), by_tile(values)
    keys_t = jnp.swapaxes(keys, 1, 2)
    values_t = jnp.swapaxes(values, 1, 2)
    qpos = jnp.transpose(coords[:, 0, :].astype(f32))
    qid = own_ids[:, None]
    kid = key_ids.reshape(tiles, 1, TILE)
    steep = math.sqrt(0.5 * LOG2E)
    lanes = lambda x: jnp.broadcast_to(x[:, None], (x.shape[0], TILE))
    cen, amp = lanes(centers), lanes(steep / widths)
    lnorm = lanes(-jnp.log2(math.sqrt(2.0 * math.pi) * widths))

    probs, att_wide, inverse_total = attention_forward(
        lo, hi, queries, keys_t, values, qpos, kpos, qid, kid, cen, amp, lnorm,
        jnp.transpose(w_pair), head_dim,
    )
    attended = unpadded(att_wide, 1)
    att_low = attended.astype(bf16)
    after_att = base_rows + jnp.dot(att_low, w_out_full, preferred_element_type=f32)
    normed_two, inverse_two = norm_parts(after_att)
    ffn_in = (normed_two * gain_two + shift_two).astype(bf16)
    hidden = jnp.dot(ffn_in, w_up_full, preferred_element_type=f32)
    activated_full, gelu_pull = jax.vjp(gelu_tanh, hidden)
    activated = activated_full.astype(bf16)
    block_sum = after_att + jnp.dot(activated, w_down_full, preferred_element_type=f32)
    out_low = block_sum.astype(bf16)
    force_rows = along_rows(w_force, out_low)
    force_cot = force_grad[:, 0, :]
    grad_sum = out_grad[0].astype(f32) + lax.dot_general(
        force_cot,
        w_force.astype(f32),
        (((0,), (0,)), ((), ())),
        precision=HIGHEST,
        preferred_element_type=f32,
    )
    grad_force = jnp.dot(
        force_cot, out_low.astype(f32), precision=HIGHEST, preferred_element_type=f32
    )
    grad_sum_low = grad_sum.astype(bf16)
    grad_act_low = along_rows(grad_sum_low, w_down_full).astype(bf16)
    grad_hidden_low = gelu_pull(grad_act_low.astype(f32))[0].astype(bf16)
    grad_ffn_in = along_rows(grad_hidden_low, w_up_full)
    grad_norm_two, grad_gain_two, grad_shift_two = norm_back(
        grad_ffn_in, normed_two, inverse_two, gain_two
    )
    grad_after = grad_sum + grad_norm_two
    grad_after_low = grad_after.astype(bf16)
    grad_att_low = along_rows(grad_after_low, w_out_full).astype(bf16)

    def my_half(x):
        half = x.shape[1] // 2
        return jnp.where(my_core == 0, x[:, :half], x[:, half:])

    def other_half(x):
        half = x.shape[1] // 2
        return jnp.where(my_core == 0, x[:, half:], x[:, :half])

    def both_cores(left, right):
        lefts = jnp.concatenate([my_half(left), swap_cores(other_half(left))], axis=0)
        rights = jnp.concatenate([right, swap_cores(right)], axis=0)
        return lefts, rights

    def weight_grads(pairs):
        pieces = []
        for left, right in pairs:
            lefts, rights = both_cores(left, right)
            for at in range(0, lefts.shape[1], model_width // 2):
                piece = cross_rows(rights, lefts[:, at : at + model_width // 2])
                pieces.append(piece.astype(bf16).reshape(row_size, -1, model_width // 2))
        return jnp.concatenate(pieces, axis=1)

    ffn_grads = weight_grads(
        [(ffn_in, grad_hidden_low), (att_low, grad_after_low), (activated, grad_sum_low)]
    )

    def split_grads(total):
        up, out = w_up.shape[1] // row_size, w_out.shape[1] // row_size
        down = total[up + out :].reshape(-1, out, model_width // 2)
        return (
            jnp.transpose(total[:up]),
            jnp.transpose(total[up : up + out]),
            jnp.transpose(jnp.concatenate([x for x in down], axis=1)),
        )

    outer, inner = my_index // INNER, my_index % INNER
    outers = row_size // INNER

    def by_plane(x, which):
        return lax.dynamic_index_in_dim(x.reshape((outers, INNER) + x.shape[1:]), which, 1, False)

    def to_planes():
        arrived = []
        for flip in (1, 2, 3):
            pairs = [(r, r ^ flip) for r in range(row_size)]
            arrived.append(lax.ppermute(by_plane(ffn_grads, inner ^ flip), "row", pairs))
        return arrived

    def plane_sums(arrived):
        total = by_plane(ffn_grads, inner).astype(f32)
        for some in arrived:
            total = total + some.astype(f32)
        own = lax.dynamic_index_in_dim(total, outer, 0, False)
        others = [
            lax.dynamic_index_in_dim(total, (outer + step) % outers, 0, False).astype(bf16)
            for step in range(1, outers)
        ]
        return own, others

    def to_columns(others):
        arrived = []
        for step in range(1, outers):
            pairs = [
                (r, ((r // INNER + step) % outers) * INNER + r % INNER) for r in range(row_size)
            ]
            arrived.append(lax.ppermute(others[step - 1], "row", pairs))
        return arrived

    def over_rows(x):
        return jnp.transpose(
            lax.psum_scatter(x, "row", scatter_dimension=0, tiled=False).astype(f32)
        )

    do_wide = padded(grad_att_low, 1)
    do_wide, ffn_grads = lax.optimization_barrier((do_wide, ffn_grads))
    if covers:
        arrived = to_planes()
    else:
        summed = lax.psum_scatter(ffn_grads, "row", scatter_dimension=0, tiled=False).astype(f32)

    dq, dkt, dvt, pair_t, kernel_sums = attention_backward(
        lo, hi, probs, inverse_total, queries, do_wide, att_wide, keys, values_t,
        qpos, kpos, cen, amp, lnorm, w_pair, head_dim,
    )
    if covers:
        dq, arrived = lax.optimization_barrier((dq, arrived))
        own_sum, others = plane_sums(arrived)
        dq, others = lax.optimization_barrier((dq, others))
        far_sums = to_columns(others)
        grad_normed_in, w_qkv_grad_t = finish_rows(
            dkt, dvt, dq, every, normed_in, w_q, w_k, w_v, row_size, head_dim
        )
        grad_normed_in, far_sums = lax.optimization_barrier((grad_normed_in, far_sums))
        summed = own_sum + sum(x.astype(f32) for x in far_sums)
        w_qkv_grad = jnp.transpose(w_qkv_grad_t)
    else:
        key_grad, value_grad = jnp.transpose(dkt), jnp.transpose(dvt)
        grad_every = along_rows(key_grad, w_k) + along_rows(value_grad, w_v)
        grad_normed_in = along_rows(dq, w_q) + send_back(grad_every)
        parts = [(normed_in, dq), (every, key_grad), (every, value_grad)]
        whole_grad = jnp.concatenate(
            [unpadded(cross_rows(right, left), 0) for left, right in parts], axis=0
        ).astype(bf16)
        half_grad = lax.psum_scatter(whole_grad, "wt", scatter_dimension=1, tiled=True)
        w_qkv_grad = over_rows(half_grad.reshape(row_size, -1, half_grad.shape[1]))
    w_up_grad, w_out_grad, w_down_grad = split_grads(summed)
    grad_norm_one, grad_gain_one, grad_shift_one = norm_back(
        grad_normed_in, normed_one, inverse_one, gain_one
    )
    atoms_grad = grad_after + grad_norm_one
    grad_table = lax.dot_general(
        onehot.astype(f32),
        atoms_grad,
        (((0,), (0,)), ((), ())),
        precision=HIGHEST,
        preferred_element_type=f32,
    )
    sums = jnp.sum(kernel_sums, axis=2)
    center_part = sums[1] / (steep * widths)
    width_part = (sums[2] / (steep * steep) - sums[0]) / widths
    small = (
        grad_table,
        grad_gain_one,
        grad_shift_one,
        center_part,
        width_part,
        jnp.transpose(pair_t),
        grad_gain_two,
        grad_shift_two,
        grad_force,
    )
    if covers:
        flat = jnp.concatenate([x.reshape(-1) for x in small])
        devices = row_size * lax.axis_size("wt")
        piece = -(-flat.shape[0] // (devices * 8 * 128)) * 128
        flat = jnp.pad(flat, (0, devices * 8 * piece - flat.shape[0]))
        flat = total_over_all(flat.reshape(devices, 8, piece)).reshape(-1)
        small_sums, at = [], 0
        for x in small:
            small_sums.append(flat[at : at + x.size].reshape(x.shape))
            at += x.size
    else:
        small_sums = lax.psum(small, ("row", "wt"))
    return (
        out_low[None],
        force_rows[:, None, :],
        atoms_grad[None],
        small_sums[0],
        small_sums[1],
        small_sums[2],
        w_qkv_grad,
        small_sums[3],
        small_sums[4],
        small_sums[5],
        w_out_grad,
        small_sums[6],
        small_sums[7],
        w_up_grad,
        w_down_grad,
        small_sums[8],
    )


def solution(mesh):
    in_specs = (
        P("wt", "row", None),
        P(None, "wt", "row"),
        P("wt", "row"),
        P("wt", None),
        P("wt"),
        P(),
        P(),
        P(),
        P("wt", None),
        P(),
        P(),
        P(),
        P("wt", None),
        P(),
        P(),
        P("wt", None),
        P("wt", None),
        P(),
        P("wt", "row", None),
        P(None, "wt", "row"),
    )
    out_specs = (
        P("wt", "row", None),
        P(None, "wt", "row"),
        P("wt", "row", None),
        P(),
        P(),
        P(),
        P("wt", "row"),
        P(),
        P(),
        P(),
        P("wt", "row"),
        P(),
        P(),
        P("wt", "row"),
        P("wt", "row"),
        P(),
    )
    return jax.shard_map(
        on_device, mesh=mesh, in_specs=in_specs, out_specs=out_specs, check_vma=False
    )
```

```python
import functools
import math

import jax
import jax.numpy as jnp
from jax import lax
from jax.experimental import pallas as pl
from jax.experimental.pallas import tpu as pltpu
from jax.sharding import PartitionSpec as P

MAXLEN = 1024
NEG_FILL = -1e30
HIGHEST = lax.Precision.HIGHEST
QB = 32
TILE = 128
HG = 8
GW = 256
LOG2E = 1.4426950408889634
bf16 = jnp.bfloat16
f32 = jnp.float32


def shifted(x, axis, by):
    length = lax.axis_size(axis)
    pairs = [(i, i + by) for i in range(length) if 0 <= i + by < length]
    return lax.ppermute(x, axis, pairs)


def swap_cores(x):
    return lax.ppermute(x, "wt", [(0, 1), (1, 0)])


def norm_parts(values_in):
    average = jnp.mean(values_in, axis=-1, keepdims=True)
    centred = values_in - average
    inverse = lax.rsqrt(jnp.mean(centred * centred, axis=-1, keepdims=True) + 1e-05)
    return (centred * inverse, inverse)


def norm_back(grad_out, normed, inverse, gain_vec):
    grad_normed = grad_out * gain_vec
    mean_grad = jnp.mean(grad_normed, axis=-1, keepdims=True)
    mean_mixed = jnp.mean(grad_normed * normed, axis=-1, keepdims=True)
    grad_in = inverse * (grad_normed - mean_grad - normed * mean_mixed)
    return (grad_in, jnp.sum(grad_out * normed, axis=0), jnp.sum(grad_out, axis=0))


def gelu_tanh(values_in):
    return (
        0.5
        * values_in
        * (
            1.0
            + jnp.tanh(
                0.7978845608028654 * (values_in + 0.044715 * values_in * values_in * values_in)
            )
        )
    )


def time_code(moment, model_width):
    half_width = model_width // 2
    frequency = jnp.exp(-math.log(10000.0) * jnp.arange(half_width, dtype=jnp.float32) / half_width)
    angles = 100.0 * moment * frequency
    return jnp.concatenate([jnp.sin(angles), jnp.cos(angles)])


def item_ids(places, item_ends):
    return jnp.sum((places[:, None] >= item_ends[None, :]).astype(jnp.int32), axis=1)


def cross_rows(left_side, right_side):
    return lax.dot_general(
        left_side, right_side, (((0,), (0,)), ((), ())), preferred_element_type=jnp.float32
    )


def along_rows(left_side, right_side):
    return lax.dot_general(
        left_side, right_side, (((1,), (1,)), ((), ())), preferred_element_type=jnp.float32
    )


def head_mask(groups_dim):
    h = lax.broadcasted_iota(jnp.int32, (HG, GW), 0)
    f = lax.broadcasted_iota(jnp.int32, (HG, GW), 1)
    lo = h * groups_dim
    return (f >= lo) & (f < lo + groups_dim)


def expand(rows, mask):
    parts = [
        jnp.where(mask, jnp.broadcast_to(rows[i : i + 1, :], (HG, GW)), 0.0)
        for i in range(rows.shape[0])
    ]
    return jnp.concatenate(parts, axis=0)


def collapse(stacked, mask):
    count = stacked.shape[0] // HG
    parts = [
        jnp.sum(jnp.where(mask, stacked[i * HG : (i + 1) * HG, :], 0.0), axis=0, keepdims=True)
        for i in range(count)
    ]
    return jnp.concatenate(parts, axis=0)


def tile_distance(qpos_ref, kpos_ref, tile):
    total = None
    for axis in range(3):
        differ = qpos_ref[:, axis : axis + 1] - kpos_ref[tile, axis : axis + 1, :]
        total = differ * differ if total is None else total + differ * differ
    return jnp.sqrt(total)


def fwd_kernel(
    head_dim, lo_ref, hi_ref, q_ref, kt_ref, v_ref, qpos_ref, kpos_ref, qid_ref, kid_ref,
    cen_ref, amp_ref, lnorm_ref, wpt_ref, p_ref, o_ref, rl_ref,
    qexp, score, top, dist, neg, kern, bias, acc, total,
):
    block = pl.program_id(0)
    lo, hi = lo_ref[block], hi_ref[block]
    groups = wpt_ref.shape[0] // HG
    rows = QB * HG
    scale = head_dim ** (-0.5)
    mask = head_mask(head_dim)
    for g in range(groups):
        qexp[g] = expand(q_ref[:, g * GW : (g + 1) * GW].astype(f32), mask).astype(bf16)
        acc[g] = jnp.zeros((rows, GW), f32)
    top[...] = jnp.full(top.shape, NEG_FILL, f32)
    total[...] = jnp.zeros(total.shape, f32)

    def first(tile, carry):
        dist[...] = tile_distance(qpos_ref, kpos_ref, tile)
        neg[...] = jnp.where(qid_ref[:, 0:1] == kid_ref[tile], 0.0, NEG_FILL)

        def some_kernels(cg, carry):
            at = pl.ds(pl.multiple_of(cg * 16, 16), 16)
            cen, amp, lnorm = cen_ref[at, :], amp_ref[at, :], lnorm_ref[at, :]
            for i in range(QB):
                t = (dist[i : i + 1, :] - cen) * amp
                kern[at, i * TILE : (i + 1) * TILE] = jnp.exp2(lnorm - t * t).astype(bf16)
            return carry

        lax.fori_loop(0, cen_ref.shape[0] // 16, some_kernels, 0)
        for part in range(QB // 8):
            at = slice(part * 8 * TILE, (part + 1) * 8 * TILE)
            bias[:, at] = jnp.dot(wpt_ref[...], kern[:, at], preferred_element_type=f32)
        for g in range(groups):
            dots = jnp.dot(qexp[g], kt_ref[tile, g * GW : (g + 1) * GW, :], preferred_element_type=f32)
            for i in range(QB):
                here = slice(g * rows + i * HG, g * rows + (i + 1) * HG)
                value = (
                    dots[i * HG : (i + 1) * HG, :] * scale
                    + bias[g * HG : (g + 1) * HG, i * TILE : (i + 1) * TILE]
                    + neg[i : i + 1, :]
                )
                score[tile, here, :] = value
                top[here, :] = jnp.maximum(top[here, :], value)
        return carry

    lax.fori_loop(lo, hi, first, 0)
    top[...] = jnp.broadcast_to(jnp.max(top[...], axis=1, keepdims=True), top.shape)

    def second(tile, carry):
        for g in range(groups):
            here = slice(g * rows, (g + 1) * rows)
            prob = jnp.exp(score[tile, here, :] - top[here, :])
            total[here, :] += prob
            low = prob.astype(bf16)
            p_ref[0, tile, here, :] = low
            acc[g] += jnp.dot(low, v_ref[tile, :, g * GW : (g + 1) * GW], preferred_element_type=f32)
        return carry

    lax.fori_loop(lo, hi, second, 0)
    for g in range(groups):
        here = slice(g * rows, (g + 1) * rows)
        inverse = 1.0 / jnp.sum(total[here, :], axis=1, keepdims=True)
        rl_ref[here, :] = jnp.broadcast_to(inverse, (rows, TILE))
        o_ref[:, g * GW : (g + 1) * GW] = collapse(acc[g] * inverse, mask)


def bwd_kernel(
    head_dim, lo_ref, hi_ref, p_ref, rl_ref, q_ref, do_ref, o_ref, k_ref, vt_ref, qpos_ref, kpos_ref,
    cen_ref, amp_ref, lnorm_ref, wp_ref, dq_ref, dkt_ref, dvt_ref, m0_ref, sums_ref,
    qext, doexp, doext, delta, dqacc, glow, dist, kern, gk, dkt_acc, dvt_acc,
):
    block = pl.program_id(0)
    lo, hi = lo_ref[block], hi_ref[block]
    groups = q_ref.shape[1] // GW
    rows = QB * HG
    scale = head_dim ** (-0.5)
    used = head_dim * HG
    mask = head_mask(head_dim)

    @pl.when(block == 0)
    def _():
        dkt_acc[...] = jnp.zeros(dkt_acc.shape, f32)
        dvt_acc[...] = jnp.zeros(dvt_acc.shape, f32)
        m0_ref[...] = jnp.zeros(m0_ref.shape, f32)
        sums_ref[...] = jnp.zeros(sums_ref.shape, f32)

    for g in range(groups):
        lanes = slice(g * GW, (g + 1) * GW)
        here = slice(g * rows, (g + 1) * rows)
        inverse = rl_ref[here, 0:1]
        qext[g] = jnp.transpose(expand(q_ref[:, lanes].astype(f32), mask))[:used, :].astype(bf16)
        grads = do_ref[:, lanes].astype(f32)
        both = expand(grads, mask) * inverse
        doexp[g] = both.astype(bf16)
        doext[g] = jnp.transpose(both)[:used, :].astype(bf16)
        mixed = jnp.sum(expand(grads * o_ref[:, lanes], mask), axis=1, keepdims=True) * inverse
        delta[here, :] = jnp.broadcast_to(mixed, (rows, TILE))
        dqacc[g] = jnp.zeros((rows, GW), f32)

    def one_tile(tile, carry):
        keys = pl.ds(pl.multiple_of(tile * TILE, TILE), TILE)
        dist[...] = tile_distance(qpos_ref, kpos_ref, tile)
        for pair in range(groups // 2):
            grads = []
            for g in (2 * pair, 2 * pair + 1):
                lanes = slice(g * GW, (g + 1) * GW)
                here = slice(g * rows, (g + 1) * rows)
                feats = slice(g * used, (g + 1) * used)
                low = p_ref[0, tile, here, :]
                dp = jnp.dot(doexp[g], vt_ref[tile, lanes, :], preferred_element_type=f32)
                gl = low.astype(f32) * (dp - delta[here, :])
                grads.append(gl)
                gl_low = gl.astype(bf16)
                dqacc[g] += jnp.dot(gl_low, k_ref[tile, :, lanes], preferred_element_type=f32)
                dkt_acc[feats, keys] += jnp.dot(qext[g], gl_low, preferred_element_type=f32)
                dvt_acc[feats, keys] += jnp.dot(doext[g], low, preferred_element_type=f32)
            for i in range(QB):
                at = slice(i * HG, (i + 1) * HG)
                glow[pair * 16 : (pair + 1) * 16, i * TILE : (i + 1) * TILE] = jnp.concatenate(
                    [grads[0][at, :], grads[1][at, :]], axis=0
                ).astype(bf16)
        for part in range(QB // 8):
            at = slice(part * 8 * TILE, (part + 1) * 8 * TILE)
            gk[:, at] = jnp.dot(wp_ref[...], glow[:, at], preferred_element_type=f32)

        def some_kernels(cg, carry):
            at = pl.ds(pl.multiple_of(cg * 16, 16), 16)
            cen, amp, lnorm = cen_ref[at, :], amp_ref[at, :], lnorm_ref[at, :]
            plain = jnp.zeros((16, TILE), f32)
            once = jnp.zeros((16, TILE), f32)
            twice = jnp.zeros((16, TILE), f32)
            for i in range(QB):
                lanes = slice(i * TILE, (i + 1) * TILE)
                t = (dist[i : i + 1, :] - cen) * amp
                value = jnp.exp2(lnorm - t * t)
                kern[at, lanes] = value.astype(bf16)
                weighted = gk[at, lanes] * value
                plain = plain + weighted
                weighted = weighted * t
                once = once + weighted
                twice = twice + weighted * t
            sums_ref[0, at, :] += plain
            sums_ref[1, at, :] += once
            sums_ref[2, at, :] += twice
            return carry

        lax.fori_loop(0, cen_ref.shape[0] // 16, some_kernels, 0)
        m0_ref[...] += lax.dot_general(
            glow[...], kern[...], (((1,), (1,)), ((), ())), preferred_element_type=f32
        )
        return carry

    lax.fori_loop(lo, hi, one_tile, 0)
    for g in range(groups):
        dq_ref[:, g * GW : (g + 1) * GW] = (collapse(dqacc[g], mask) * scale).astype(bf16)

    @pl.when(block == pl.num_programs(0) - 1)
    def _():
        dkt_ref[...] = (dkt_acc[...] * scale).astype(bf16)
        dvt_ref[...] = dvt_acc[...].astype(bf16)


def whole(shape):
    return pl.BlockSpec(shape, lambda *_: (0,) * len(shape), pipeline_mode=pl.Buffered(1))


def attention_forward(lo, hi, q, kt, v, qpos, kpos, qid, kid, cen, amp, lnorm, wpt, head_dim):
    tiles = kt.shape[0]
    wide = q.shape[1]
    groups = wide // GW
    rows = QB * HG
    blocks = q.shape[0] // QB
    kernels, heads = cen.shape[0], wpt.shape[0]
    by_block = lambda b, *_: (b, 0)
    return pl.pallas_call(
        functools.partial(fwd_kernel, head_dim),
        grid_spec=pltpu.PrefetchScalarGridSpec(
            num_scalar_prefetch=2,
            grid=(blocks,),
            in_specs=[
                pl.BlockSpec((QB, wide), by_block),
                whole(kt.shape),
                whole(v.shape),
                pl.BlockSpec((QB, 3), by_block),
                whole(kpos.shape),
                pl.BlockSpec((QB, 1), by_block),
                whole(kid.shape),
                whole(cen.shape),
                whole(amp.shape),
                whole(lnorm.shape),
                whole(wpt.shape),
            ],
            out_specs=[
                pl.BlockSpec((1, tiles, groups * rows, TILE), lambda b, *_: (b, 0, 0, 0)),
                pl.BlockSpec((QB, wide), by_block),
                pl.BlockSpec((groups * rows, TILE), by_block),
            ],
            scratch_shapes=[
                pltpu.VMEM((groups, rows, GW), bf16),
                pltpu.VMEM((tiles, groups * rows, TILE), f32),
                pltpu.VMEM((groups * rows, TILE), f32),
                pltpu.VMEM((QB, TILE), f32),
                pltpu.VMEM((QB, TILE), f32),
                pltpu.VMEM((kernels, QB * TILE), bf16),
                pltpu.VMEM((heads, QB * TILE), f32),
                pltpu.VMEM((groups, rows, GW), f32),
                pltpu.VMEM((groups * rows, TILE), f32),
            ],
        ),
        out_shape=[
            jax.ShapeDtypeStruct((blocks, tiles, groups * rows, TILE), bf16),
            jax.ShapeDtypeStruct(q.shape, f32),
            jax.ShapeDtypeStruct((blocks * groups * rows, TILE), f32),
        ],
        compiler_params=pltpu.CompilerParams(vmem_limit_bytes=60 << 20),
        cost_estimate=pl.CostEstimate(
            flops=30_000_000_000, bytes_accessed=40_000_000, transcendentals=200_000_000
        ),
        name="attend",
    )(lo, hi, q, kt, v, qpos, kpos, qid, kid, cen, amp, lnorm, wpt)


def attention_backward(lo, hi, p, rl, q, do, o, k, vt, qpos, kpos, cen, amp, lnorm, wp, head_dim):
    tiles = vt.shape[0]
    wide = q.shape[1]
    groups = wide // GW
    rows = QB * HG
    blocks = q.shape[0] // QB
    kernels, heads = wp.shape
    used = HG * head_dim
    by_block = lambda b, *_: (b, 0)
    return pl.pallas_call(
        functools.partial(bwd_kernel, head_dim),
        grid_spec=pltpu.PrefetchScalarGridSpec(
            num_scalar_prefetch=2,
            grid=(blocks,),
            in_specs=[
                pl.BlockSpec((1, tiles, groups * rows, TILE), lambda b, *_: (b, 0, 0, 0)),
                pl.BlockSpec((groups * rows, TILE), by_block),
                pl.BlockSpec((QB, wide), by_block),
                pl.BlockSpec((QB, wide), by_block),
                pl.BlockSpec((QB, wide), by_block),
                whole(k.shape),
                whole(vt.shape),
                pl.BlockSpec((QB, 3), by_block),
                whole(kpos.shape),
                whole(cen.shape),
                whole(amp.shape),
                whole(lnorm.shape),
                whole(wp.shape),
            ],
            out_specs=[
                pl.BlockSpec((QB, wide), by_block),
                whole((groups * used, tiles * TILE)),
                whole((groups * used, tiles * TILE)),
                whole((heads, kernels)),
                whole((3, kernels, TILE)),
            ],
            scratch_shapes=[
                pltpu.VMEM((groups, used, rows), bf16),
                pltpu.VMEM((groups, rows, GW), bf16),
                pltpu.VMEM((groups, used, rows), bf16),
                pltpu.VMEM((groups * rows, TILE), f32),
                pltpu.VMEM((groups, rows, GW), f32),
                pltpu.VMEM((heads, QB * TILE), bf16),
                pltpu.VMEM((QB, TILE), f32),
                pltpu.VMEM((kernels, QB * TILE), bf16),
                pltpu.VMEM((kernels, QB * TILE), f32),
                pltpu.VMEM((groups * used, tiles * TILE), f32),
                pltpu.VMEM((groups * used, tiles * TILE), f32),
            ],
        ),
        out_shape=[
            jax.ShapeDtypeStruct(q.shape, bf16),
            jax.ShapeDtypeStruct((groups * used, tiles * TILE), bf16),
            jax.ShapeDtypeStruct((groups * used, tiles * TILE), bf16),
            jax.ShapeDtypeStruct((heads, kernels), f32),
            jax.ShapeDtypeStruct((3, kernels, TILE), f32),
        ],
        compiler_params=pltpu.CompilerParams(vmem_limit_bytes=62 << 20),
        cost_estimate=pl.CostEstimate(
            flops=60_000_000_000, bytes_accessed=60_000_000, transcendentals=200_000_000
        ),
        name="attend_back",
    )(lo, hi, p, rl, q, do, o, k, vt, qpos, kpos, cen, amp, lnorm, wp)


MESH = pl.DeviceIdType.MESH
INNER = 4


def places():
    row, core = lax.axis_index("row"), lax.axis_index("wt")
    outer, inner = row // INNER, row % INNER
    return row, core, outer, inner


def plane_mates(inner):
    y, x = inner // 2, inner % 2
    return (y * 2 + (1 - x), (1 - y) * 2 + x, (1 - y) * 2 + (1 - x))


def greet(targets):
    barrier = pltpu.get_barrier_semaphore()
    for target in targets:
        pl.semaphore_signal(barrier, inc=1, device_id=target, device_id_type=MESH)
    pl.semaphore_wait(barrier, len(targets))


def remote(src, dst, send_sem, recv_sem, target):
    return pltpu.make_async_remote_copy(
        src_ref=src, dst_ref=dst, send_sem=send_sem, recv_sem=recv_sem,
        device_id=target, device_id_type=MESH,
    )


def front_kernel(
    atoms_ref, og_ref, sm_ref, c_ref, w_ref, code_ref, table_ref, gain_ref, shift_ref,
    base_ref, ogo_ref, smo_ref, every_ref, co_ref, wo_ref, wq_ref, q_ref, k_ref, kt_ref, v_ref, vt_ref,
    dealt, own, wpad, k_st, kt_st, v_st, vt_st,
    deal_s, deal_r, w_sems, sends, gets, sends_c, gets_c, outs,
):
    row, core, outer, inner = places()
    outers, shards = every_ref.shape[0], every_ref.shape[1]
    width = own.shape[2]
    groups = q_ref.shape[1] // GW
    used = width // groups
    mates = plane_mates(inner)
    far = [(outer + step) % outers for step in range(1, outers)]
    plane = [(outer * INNER + mate, core) for mate in mates]
    column = [(other * INNER + inner, core) for other in far]
    barrier = pltpu.get_barrier_semaphore()
    for target in plane + column + [(row, 1 - core)]:
        pl.semaphore_signal(barrier, inc=1, device_id=target, device_id_type=MESH)
    for m in range(outers):
        @pl.when(m * INNER + outer != row)
        def _():
            pl.semaphore_signal(
                barrier, inc=1, device_id=(m * INNER + outer, core), device_id_type=MESH
            )
    pl.semaphore_wait(barrier, outers + 2 * INNER - 1 - jnp.where(outer == inner, 1, 0))

    dealing = ((atoms_ref, dealt), (sm_ref, smo_ref), (og_ref, ogo_ref))

    def deal(q, slot, target, which=(0, 1, 2)):
        return [
            remote(
                dealing[at][0].at[q], dealing[at][1].at[slot], deal_s.at[q, at], deal_r.at[slot, at],
                (target, core),
            )
            for at in which
        ]

    for q in range(INNER):
        target = inner * INNER + q

        @pl.when(target != row)
        def _():
            for copy in deal(q, outer, target):
                copy.start()

        @pl.when(target == row)
        def _():
            dealt[outer] = atoms_ref[q]
            smo_ref[outer] = sm_ref[q]
            ogo_ref[outer] = og_ref[q]

    to_core = remote(w_ref, wo_ref.at[core], w_sems.at[0], w_sems.at[1], (row, 1 - core))
    to_core.start()
    wo_ref[core] = w_ref[...]
    co_ref[row] = c_ref[...]
    wpad[...] = jnp.zeros(wpad.shape, bf16)

    for m in range(outers):
        @pl.when(m * INNER + outer != row)
        def _():
            for copy in deal(0, m, m * INNER + outer, (0, 1)):
                copy.wait_recv()

    small = smo_ref[0]
    for m in range(1, outers):
        small = small + smo_ref[m]
    kinds = lax.broadcasted_iota(jnp.int32, (table_ref.shape[0], own.shape[0] * own.shape[1]), 0)
    hot = jnp.where(kinds.astype(f32) == small[0:1, :], 1.0, 0.0).astype(bf16)
    base = (
        dealt[...].astype(f32).reshape(base_ref.shape)
        + code_ref[...]
        + lax.dot_general(hot, table_ref[...], (((0,), (0,)), ((), ())), preferred_element_type=f32)
    )
    base_ref[...] = base
    normed, _ = norm_parts(base)
    normed_in = (normed * gain_ref[...] + shift_ref[...]).astype(bf16)
    own[...] = normed_in.reshape(own.shape)
    every_ref[:, row] = own[...]
    started = []

    def send(src, src_c, slot, target):
        at = len(started) // 2
        for copy in (
            remote(src, every_ref.at[:, slot], sends.at[at], gets.at[slot], target),
            remote(src_c, co_ref.at[slot], sends_c.at[at], gets_c.at[slot], target),
        ):
            copy.start()
            started.append(copy)

    for target in column + plane:
        send(own, c_ref, row, target)

    to_core.wait_recv()
    for half in range(2):
        here = slice(half * w_ref.shape[0], (half + 1) * w_ref.shape[0])
        for part in range(3):
            for g in range(groups):
                lane = part * width + g * used
                first, last = lane // 128 * 128, -(-(lane + used) // 128) * 128
                piece = wo_ref[half, :, first:last]
                wpad[here, part * groups * GW + g * GW : part * groups * GW + g * GW + used] = piece[
                    :, lane - first : lane - first + used
                ]

    def arrived(slot):
        remote(own, every_ref.at[:, slot], sends.at[0], gets.at[slot], (row, core)).wait_recv()
        remote(c_ref, co_ref.at[slot], sends_c.at[0], gets_c.at[slot], (row, core)).wait_recv()

    for step in range(1, outers):
        slot = ((outer + outers - step) % outers) * INNER + inner
        arrived(slot)
        for target in plane:
            send(every_ref.at[:, slot], co_ref.at[slot], slot, target)

    wide = groups * GW
    wq_ref[...] = wpad[:, :wide]
    q_ref[...] = jnp.dot(
        own[...].reshape(base_ref.shape), wpad[:, :wide], preferred_element_type=f32
    ).astype(bf16)

    def store(slot, tile):
        return [
            pltpu.make_async_copy(src.at[slot], dst.at[tile], outs.at[slot, at])
            for at, (src, dst) in enumerate(((k_st, k_ref), (kt_st, kt_ref), (v_st, v_ref), (vt_st, vt_ref)))
        ]

    def project(step, carry):
        a = (outer + outers - step // outers) % outers
        m = step % outers
        tile = m * INNER + a
        slot = step % 2

        @pl.when(m == 0)
        def _():
            for mate in mates:
                arrived(a * INNER + mate)

        @pl.when(step >= 2)
        def _():
            for copy in store(slot, tile):
                copy.wait()

        x = every_ref[m, pl.ds(a * INNER, INNER)].reshape(base_ref.shape)
        key = jnp.dot(x, wpad[:, wide : 2 * wide], preferred_element_type=f32)
        k_st[slot] = key.astype(bf16)
        kt_st[slot] = jnp.transpose(key).astype(bf16)
        value = jnp.dot(x, wpad[:, 2 * wide :], preferred_element_type=f32)
        v_st[slot] = value.astype(bf16)
        vt_st[slot] = jnp.transpose(value).astype(bf16)
        for copy in store(slot, tile):
            copy.start()
        return carry

    lax.fori_loop(0, shards, project, 0)
    for slot in range(2):
        for copy in store(slot, slot):
            copy.wait()
    for m in range(outers):
        @pl.when(m * INNER + outer != row)
        def _():
            for copy in deal(0, m, m * INNER + outer, (2,)):
                copy.wait_recv()
    for q in range(INNER):
        @pl.when(inner * INNER + q != row)
        def _():
            for copy in deal(q, outer, inner * INNER + q):
                copy.wait_send()
    to_core.wait_send()
    for copy in started:
        copy.wait_send()


def front(atoms, og, sm, c, w_half, code, table, gain, shift, rows, heads):
    outers = rows // INNER
    count = (outers - 1) + 3 * outers
    quarter, width = atoms.shape[1:]
    total = INNER * quarter
    wide = heads // HG * GW
    tiles = rows * total // TILE
    vmem = pl.BlockSpec(memory_space=pltpu.VMEM)
    hbm = pl.BlockSpec(memory_space=pl.ANY)
    shape = jax.ShapeDtypeStruct
    return pl.pallas_call(
        front_kernel,
        out_shape=[
            shape((total, width), f32),
            shape(og.shape, bf16),
            shape(sm.shape, f32),
            shape((outers, rows, quarter, width), bf16),
            shape((rows,) + c.shape, bf16),
            shape((2,) + w_half.shape, bf16),
            shape((width, wide), bf16),
            shape((total, wide), bf16),
            shape((tiles, TILE, wide), bf16),
            shape((tiles, wide, TILE), bf16),
            shape((tiles, TILE, wide), bf16),
            shape((tiles, wide, TILE), bf16),
        ],
        in_specs=[vmem] * 9,
        out_specs=[vmem] * 8 + [hbm] * 4,
        scratch_shapes=[
            pltpu.VMEM((outers, quarter, width), bf16),
            pltpu.VMEM((outers, quarter, width), bf16),
            pltpu.VMEM((width, 3 * wide), bf16),
            pltpu.VMEM((2, TILE, wide), bf16),
            pltpu.VMEM((2, wide, TILE), bf16),
            pltpu.VMEM((2, TILE, wide), bf16),
            pltpu.VMEM((2, wide, TILE), bf16),
            pltpu.SemaphoreType.DMA((INNER, 3)),
            pltpu.SemaphoreType.DMA((outers, 3)),
            pltpu.SemaphoreType.DMA((2,)),
            pltpu.SemaphoreType.DMA((count,)),
            pltpu.SemaphoreType.DMA((rows,)),
            pltpu.SemaphoreType.DMA((count,)),
            pltpu.SemaphoreType.DMA((rows,)),
            pltpu.SemaphoreType.DMA((2, 4)),
        ],
        compiler_params=pltpu.CompilerParams(
            collective_id=0, has_side_effects=True, vmem_limit_bytes=60 << 20
        ),
        name="front",
    )(atoms, og, sm, c, w_half, code, table, gain, shift)


def finish_kernel(outers, part_width, dkt_ref, dvt_ref, dq_ref, every_ref, own_ref, wq_ref, w_ref, xo_ref, wo_ref,
                  xs, xa, xm, xb, wp, wi, wa, wm, wb, w0_sems, a_send, a_recv, b_send, b_recv):
    row, core, outer, inner = places()
    mates = plane_mates(inner)
    count, width = own_ref.shape
    half = width // 2
    used = part_width * 8
    rows_each = wo_ref.shape[0]
    plane = [(outer * INNER + mate, core) for mate in mates]
    far = [(outer + step) % outers for step in range(1, outers)]
    column = [(other * INNER + inner, core) for other in far]
    order = far + [outer]
    greet(plane + column + [(row, 1 - core)])
    started = []

    quarter = count // INNER

    def grad_tile(tile):
        at = pl.ds(pl.multiple_of(tile * TILE, TILE), TILE)
        flipped = jnp.dot(w_ref[:, width : 2 * width], dkt_ref[:, at], preferred_element_type=f32)
        flipped += jnp.dot(w_ref[:, 2 * width :], dvt_ref[:, at], preferred_element_type=f32)
        return jnp.transpose(flipped).astype(bf16)

    def grad_plane(o):
        def one(m, carry):
            block = grad_tile(m * INNER + o)
            for i in range(INNER):
                xs[o, i, pl.ds(pl.multiple_of(m * quarter, quarter), quarter), :] = block[
                    i * quarter : (i + 1) * quarter, :
                ]
            return carry

        lax.fori_loop(0, outers, one, 0)

    def begin(copy):
        copy.start()
        started.append(copy)

    def to_mate(which, at, o, p, src, dst):
        return remote(src, dst, a_send.at[which, p, at], a_recv.at[which, p, o], plane[p])

    for at, o in enumerate(order):
        grad_plane(o)
        for p in range(3):
            begin(to_mate(0, at, o, p, xs.at[o, mates[p]], xa.at[p, o]))
    def key_part(index, carry):
        g = index
        here = pl.ds(pl.multiple_of(g * used, 16), used)
        there = pl.ds(pl.multiple_of(g * used, 16), used)
        wp[there, :] = lax.dot_general(
            dq_ref[:, pl.ds(pl.multiple_of(g * GW, GW), GW)], own_ref[...], (((0,), (0,)), ((), ())),
            preferred_element_type=f32,
        )[:used, :].astype(bf16)
        there = pl.ds(pl.multiple_of(width + g * used, 16), used)
        wp[there, :] = jnp.dot(dkt_ref[here, :], every_ref[...], preferred_element_type=f32).astype(bf16)
        there = pl.ds(pl.multiple_of(2 * width + g * used, 16), used)
        wp[there, :] = jnp.dot(dvt_ref[here, :], every_ref[...], preferred_element_type=f32).astype(bf16)
        return carry

    lax.fori_loop(0, width // used, key_part, 0)
    other_lanes = pl.ds(pl.multiple_of((1 - core) * half, 128), half)
    own_lanes = pl.ds(pl.multiple_of(core * half, 128), half)
    halves = remote(wp.at[:, other_lanes], wi, w0_sems.at[0], w0_sems.at[1], (row, 1 - core))
    halves.start()

    def plane_sum(which, own, got, o):
        total = own.astype(f32)
        for p in range(3):
            to_mate(which, 0, o, p, got.at[p, o], got.at[p, o]).wait_recv()
            total = total + got[p, o].astype(f32)
        return total

    def to_far(which, step, stage, last):
        return remote(
            stage.at[step], last.at[step], b_send.at[which, step], b_recv.at[which, step], column[step]
        )

    for step, o in enumerate(far):
        xm[step] = plane_sum(0, xs[o, inner], xa, o).astype(bf16)
        begin(to_far(0, step, xm, xb))
    halves.wait_recv()
    wi[...] = (wp[:, own_lanes].astype(f32) + wi[...].astype(f32)).astype(bf16)

    def w_rows(slot):
        return pl.ds(pl.multiple_of(slot * rows_each, 16), rows_each)

    for at, o in enumerate(order):
        for p in range(3):
            begin(to_mate(1, at, o, p, wi.at[w_rows(o * INNER + mates[p])], wa.at[p, o]))
    flipped = lax.dot_general(
        wq_ref[...], dq_ref[...], (((1,), (1,)), ((), ())), preferred_element_type=f32
    )
    total = plane_sum(0, xs[outer, inner], xa, outer) + jnp.transpose(flipped)
    for step in range(outers - 1):
        to_far(0, step, xm, xb).wait_recv()
        total = total + xb[step].astype(f32)
    xo_ref[...] = total
    for step, o in enumerate(far):
        wm[step] = plane_sum(1, wi[w_rows(o * INNER + inner), :], wa, o).astype(bf16)
        begin(to_far(1, step, wm, wb))
    total = plane_sum(1, wi[w_rows(outer * INNER + inner), :], wa, outer)
    for step in range(outers - 1):
        to_far(1, step, wm, wb).wait_recv()
        total = total + wb[step].astype(f32)
    wo_ref[...] = total
    halves.wait_send()
    for copy in started:
        copy.wait_send()


def finish_rows(dkt, dvt, dq, every, own, w_q, w, rows, head_dim):
    outers = rows // INNER
    count, width = own.shape
    each = 3 * width // rows
    half = width // 2
    vmem = pl.BlockSpec(memory_space=pltpu.VMEM)
    return pl.pallas_call(
        functools.partial(finish_kernel, outers, head_dim),
        out_shape=[
            jax.ShapeDtypeStruct((count, width), f32),
            jax.ShapeDtypeStruct((each, half), f32),
        ],
        in_specs=[vmem] * 7,
        out_specs=[vmem] * 2,
        scratch_shapes=[
            pltpu.VMEM((outers, INNER, count, width), bf16),
            pltpu.VMEM((3, outers, count, width), bf16),
            pltpu.VMEM((outers - 1, count, width), bf16),
            pltpu.VMEM((outers - 1, count, width), bf16),
            pltpu.VMEM((3 * width, width), bf16),
            pltpu.VMEM((3 * width, half), bf16),
            pltpu.VMEM((3, outers, each, half), bf16),
            pltpu.VMEM((outers - 1, each, half), bf16),
            pltpu.VMEM((outers - 1, each, half), bf16),
            pltpu.SemaphoreType.DMA((2,)),
            pltpu.SemaphoreType.DMA((2, 3, outers)),
            pltpu.SemaphoreType.DMA((2, 3, outers)),
            pltpu.SemaphoreType.DMA((2, outers - 1)),
            pltpu.SemaphoreType.DMA((2, outers - 1)),
        ],
        compiler_params=pltpu.CompilerParams(
            collective_id=1, has_side_effects=True, vmem_limit_bytes=60 << 20
        ),
        name="finish_rows",
    )(dkt, dvt, dq, every, own, w_q, w)


def total_kernel(
    count, x_ref, ag_ref, bo_ref, fo_ref, out_ref, ago_ref, boo_ref, foo_ref,
    got, s1, r1, s2, r2, back_s, back_r,
):
    row, core, outer, inner = places()
    me = row * 2 + core
    barrier = pltpu.get_barrier_semaphore()

    def place(step):
        other = (me + step) % count
        return other, (other // 2, other % 2)

    def hello(step, carry):
        pl.semaphore_signal(barrier, inc=1, device_id=place(step)[1], device_id_type=MESH)
        return carry

    lax.fori_loop(1, count, hello, 0)
    pl.semaphore_wait(barrier, count - 1)

    def first(step):
        other, target = place(step)
        return remote(x_ref.at[other], got.at[step], s1.at[step], r1.at[step], target)

    def second(step):
        return remote(out_ref.at[me], out_ref.at[me], s2.at[step], r2.at[step], place(step)[1])

    def from_other(step):
        other = (me + count - step) % count
        return remote(out_ref.at[me], out_ref.at[other], s2.at[step], r2.at[step], place(step)[1])

    def start_first(step, carry):
        first(step).start()
        return carry

    def add(step, total):
        first(step).wait_recv()
        return total + got[step]

    def start_second(step, carry):
        second(step).start()
        return carry

    def end(step, carry):
        from_other(step).wait_recv()
        first(step).wait_send()
        second(step).wait_send()
        return carry

    def back(m, slot, target):
        return [
            remote(src, dst.at[slot], back_s.at[m, at], back_r.at[slot, at], (target, core))
            for at, (src, dst) in enumerate(
                ((ag_ref.at[m], ago_ref), (bo_ref.at[m], boo_ref), (fo_ref, foo_ref))
            )
        ]

    lax.fori_loop(1, count, start_first, 0)
    for m in range(ag_ref.shape[0]):
        owner = m * INNER + outer

        @pl.when(owner != row)
        def _():
            for copy in back(m, inner, owner):
                copy.start()

        @pl.when(owner == row)
        def _():
            ago_ref[inner] = ag_ref[m]
            boo_ref[inner] = bo_ref[m]
            foo_ref[inner] = fo_ref[...]

    out_ref[me] = lax.fori_loop(1, count, add, x_ref[me])
    lax.fori_loop(1, count, start_second, 0)
    for q in range(INNER):
        @pl.when(inner * INNER + q != row)
        def _():
            for copy in back(0, q, inner * INNER + q):
                copy.wait_recv()
    for m in range(ag_ref.shape[0]):
        @pl.when(m * INNER + outer != row)
        def _():
            for copy in back(m, inner, m * INNER + outer):
                copy.wait_send()
    lax.fori_loop(1, count, end, 0)


def total_over_all(x, ag, bo, fo):
    count = x.shape[0]
    vmem = pl.BlockSpec(memory_space=pltpu.VMEM)
    shape = jax.ShapeDtypeStruct
    return pl.pallas_call(
        functools.partial(total_kernel, count),
        out_shape=[
            shape(x.shape, f32), shape(ag.shape, f32), shape(bo.shape, bf16), shape((INNER,) + fo.shape, f32)
        ],
        in_specs=[vmem] * 4,
        out_specs=[vmem] * 4,
        scratch_shapes=[pltpu.VMEM(x.shape, f32)]
        + [pltpu.SemaphoreType.DMA((count,))] * 4
        + [pltpu.SemaphoreType.DMA((INNER, 3))] * 2,
        compiler_params=pltpu.CompilerParams(
            collective_id=2, has_side_effects=True, vmem_limit_bytes=40 << 20
        ),
        name="total_over_all",
    )(x, ag, bo, fo)


def on_device(
    atoms,
    coords,
    atom_types,
    lengths,
    times,
    type_table,
    gain_one,
    shift_one,
    w_qkv,
    centers,
    widths,
    w_pair,
    w_out,
    gain_two,
    shift_two,
    w_up,
    w_down,
    w_force,
    out_grad,
    force_grad,
):
    micro_count, row_count, model_width = atoms.shape
    head_count = w_pair.shape[1]
    head_dim = model_width // head_count
    score_scale = head_dim ** (-0.5)
    my_index = lax.axis_index("row")
    my_core = lax.axis_index("wt")
    row_size = lax.axis_size("row")
    reach_shards = (MAXLEN - 2) // row_count + 1
    all_rows = row_count * row_size
    groups = head_count // HG
    used = HG * head_dim
    dealt = row_size == INNER * INNER and row_count == INNER * QB
    covers = row_size <= 2 * reach_shards + 1
    span = row_size if covers else 2 * reach_shards + 1
    key_count = span * row_count
    key_base = 0 if covers else (my_index - reach_shards) * row_count
    type_codes = jnp.arange(type_table.shape[0], dtype=jnp.int32)

    def fetch(x, axis):
        if covers:
            return lax.all_gather(x, "row", axis=axis, tiled=True)
        far = [shifted(x, "row", by) for by in range(reach_shards, 0, -1)]
        near = [shifted(x, "row", -by) for by in range(1, reach_shards + 1)]
        return jnp.concatenate(far + [x] + near, axis=axis)

    def send_back(x):
        if covers:
            return lax.psum_scatter(x.astype(bf16), "row", scatter_dimension=0, tiled=True).astype(f32)
        shards = x.reshape(span, row_count, model_width)
        own = shards[reach_shards]
        for offset in range(1, reach_shards + 1):
            for by in (offset, -offset):
                own = own + shifted(shards[reach_shards - by].astype(bf16), "row", -by).astype(f32)
        return own

    def padded(x, axis):
        split = x.reshape(x.shape[:axis] + (groups, used) + x.shape[axis + 1 :])
        pads = [(0, 0)] * split.ndim
        pads[axis + 1] = (0, GW - used)
        return jnp.pad(split, pads).reshape(x.shape[:axis] + (groups * GW,) + x.shape[axis + 1 :])

    def unpadded(x, axis):
        split = x.reshape(x.shape[:axis] + (groups, GW) + x.shape[axis + 1 :])
        split = lax.slice_in_dim(split, 0, used, axis=axis + 1)
        return split.reshape(x.shape[:axis] + (groups * used,) + x.shape[axis + 1 :])

    w_out_full = lax.all_gather(w_out, "wt", axis=0, tiled=True)
    w_up_full = lax.all_gather(w_up, "wt", axis=0, tiled=True)
    w_down_full = lax.all_gather(w_down, "wt", axis=0, tiled=True)
    item_ends = jnp.cumsum(lengths[0])
    if dealt:
        chunk = jnp.arange(row_count, dtype=jnp.int32)
        own_places = chunk // QB * (row_size * QB) + my_index * QB + chunk % QB
    else:
        own_places = my_index * row_count + jnp.arange(row_count, dtype=jnp.int32)
    own_ids = item_ids(own_places, item_ends)
    key_places = key_base + jnp.arange(key_count, dtype=jnp.int32)
    inside = (key_places >= 0) & (key_places < all_rows)
    key_ids = jnp.where(inside, item_ids(key_places, item_ends), -1)
    first_places = own_places[::QB]
    last_places = own_places[QB - 1 :: QB]
    begins = jnp.max(jnp.where(item_ends[None, :] <= first_places[:, None], item_ends[None, :], 0), axis=1)
    ends = jnp.min(
        jnp.where(item_ends[None, :] > last_places[:, None], item_ends[None, :], all_rows), axis=1
    )
    tiles = key_count // TILE
    lo = jnp.clip((begins - key_base) // TILE, 0, tiles)
    hi = jnp.clip((ends - key_base + TILE - 1) // TILE, 0, tiles)

    wide = groups * GW
    code = time_code(times[0], model_width)
    outer, inner = my_index // INNER, my_index % INNER
    outers = row_size // INNER
    if dealt:
        quarters = lambda x: x.reshape((INNER, QB) + x.shape[1:])
        notes = jnp.concatenate(
            [atom_types[0].astype(f32)[None], force_grad[:, 0, :], jnp.zeros((4, row_count), f32)], axis=0
        )
        notes = jnp.swapaxes(notes.reshape(8, INNER, QB), 0, 1)
        lane_chunk = jnp.arange(row_count, dtype=jnp.int32) // QB
        notes = jnp.where(lane_chunk == outer, jnp.tile(notes, (1, 1, INNER)), 0.0)
        low_pos = jnp.pad(coords[:, 0, :], ((0, 13), (0, 0)))
        (
            base_rows, og_rows, notes, every, every_pos, w_qkv_full, w_q, queries, keys, keys_t, values, values_t
        ) = front(
            quarters(atoms[0]), quarters(out_grad[0]), notes, low_pos, w_qkv, code[None], type_table,
            gain_one[None], shift_one[None], row_size, head_count,
        )
        og_rows = og_rows.reshape(row_count, model_width)
        notes = jnp.sum(notes, axis=0)
        kinds, force_cot = notes[0].astype(jnp.int32), notes[1:4]
        every = every.reshape(key_count, model_width)
        w_qkv_full = w_qkv_full.reshape(model_width, 3 * model_width)
        kpos = every_pos[:, :3, :].astype(f32)
        own_pos = jnp.swapaxes(kpos, 0, 1).reshape(3, outers, row_size, QB)
        own_pos = lax.dynamic_index_in_dim(own_pos, my_index, 2, False).reshape(3, row_count)
        onehot = (kinds[:, None] == type_codes[None, :]).astype(bf16)
        normed_one, inverse_one = norm_parts(base_rows)
        normed_in = (normed_one * gain_one + shift_one).astype(bf16)
    else:
        w_qkv_full = lax.all_gather(w_qkv, "wt", axis=0, tiled=True)
        w_q = padded(w_qkv_full[:, :model_width], 1)
        w_k = padded(w_qkv_full[:, model_width : 2 * model_width], 1)
        w_v = padded(w_qkv_full[:, 2 * model_width :], 1)
        og_rows, force_cot, own_pos = out_grad[0], force_grad[:, 0, :], coords[:, 0, :].astype(f32)
        onehot = (atom_types[0][:, None] == type_codes[None, :]).astype(bf16)
        base_rows = (
            atoms[0].astype(f32) + code + jnp.dot(onehot, type_table, preferred_element_type=f32)
        )
        normed_one, inverse_one = norm_parts(base_rows)
        normed_in = (normed_one * gain_one + shift_one).astype(bf16)
        every = fetch(normed_in, 0)
        positions = fetch(coords[:, 0, :], 1).astype(f32)
        kpos = jnp.swapaxes(positions.reshape(3, tiles, TILE), 0, 1)
        queries = jnp.dot(normed_in, w_q, preferred_element_type=f32).astype(bf16)
        keys = jnp.dot(every, w_k, preferred_element_type=f32).astype(bf16)
        values = jnp.dot(every, w_v, preferred_element_type=f32).astype(bf16)
        by_tile = lambda x: x.reshape(tiles, TILE, wide)
        keys, values = by_tile(keys), by_tile(values)
        keys_t = jnp.swapaxes(keys, 1, 2)
        values_t = jnp.swapaxes(values, 1, 2)
    qpos = jnp.transpose(own_pos)
    qid = own_ids[:, None]
    kid = key_ids.reshape(tiles, 1, TILE)
    steep = math.sqrt(0.5 * LOG2E)
    lanes = lambda x: jnp.broadcast_to(x[:, None], (x.shape[0], TILE))
    cen, amp = lanes(centers), lanes(steep / widths)
    lnorm = lanes(-jnp.log2(math.sqrt(2.0 * math.pi) * widths))

    probs, att_wide, inverse_total = attention_forward(
        lo, hi, queries, keys_t, values, qpos, kpos, qid, kid, cen, amp, lnorm,
        jnp.transpose(w_pair), head_dim,
    )
    attended = unpadded(att_wide, 1)
    att_low = attended.astype(bf16)
    after_att = base_rows + jnp.dot(att_low, w_out_full, preferred_element_type=f32)
    normed_two, inverse_two = norm_parts(after_att)
    ffn_in = (normed_two * gain_two + shift_two).astype(bf16)
    hidden = jnp.dot(ffn_in, w_up_full, preferred_element_type=f32)
    activated_full, gelu_pull = jax.vjp(gelu_tanh, hidden)
    activated = activated_full.astype(bf16)
    block_sum = after_att + jnp.dot(activated, w_down_full, preferred_element_type=f32)
    out_low = block_sum.astype(bf16)
    force_rows = along_rows(w_force, out_low)
    grad_sum = og_rows.astype(f32) + lax.dot_general(
        force_cot,
        w_force.astype(f32),
        (((0,), (0,)), ((), ())),
        precision=HIGHEST,
        preferred_element_type=f32,
    )
    grad_force = jnp.dot(
        force_cot, out_low.astype(f32), precision=HIGHEST, preferred_element_type=f32
    )
    grad_sum_low = grad_sum.astype(bf16)
    grad_act_low = along_rows(grad_sum_low, w_down_full).astype(bf16)
    grad_hidden_low = gelu_pull(grad_act_low.astype(f32))[0].astype(bf16)
    grad_ffn_in = along_rows(grad_hidden_low, w_up_full)
    grad_norm_two, grad_gain_two, grad_shift_two = norm_back(
        grad_ffn_in, normed_two, inverse_two, gain_two
    )
    grad_after = grad_sum + grad_norm_two
    grad_after_low = grad_after.astype(bf16)
    grad_att_low = along_rows(grad_after_low, w_out_full).astype(bf16)

    def my_half(x):
        half = x.shape[1] // 2
        return jnp.where(my_core == 0, x[:, :half], x[:, half:])

    def other_half(x):
        half = x.shape[1] // 2
        return jnp.where(my_core == 0, x[:, half:], x[:, :half])

    def both_cores(left, right):
        lefts = jnp.concatenate([my_half(left), swap_cores(other_half(left))], axis=0)
        rights = jnp.concatenate([right, swap_cores(right)], axis=0)
        return lefts, rights

    def weight_grads(pairs):
        pieces = []
        for left, right in pairs:
            lefts, rights = both_cores(left, right)
            for at in range(0, lefts.shape[1], model_width // 2):
                piece = cross_rows(rights, lefts[:, at : at + model_width // 2])
                pieces.append(piece.astype(bf16).reshape(row_size, -1, model_width // 2))
        return jnp.concatenate(pieces, axis=1)

    ffn_grads = weight_grads(
        [(ffn_in, grad_hidden_low), (att_low, grad_after_low), (activated, grad_sum_low)]
    )

    def split_grads(total):
        up, out = w_up.shape[1] // row_size, w_out.shape[1] // row_size
        down = total[up + out :].reshape(-1, out, model_width // 2)
        return (
            jnp.transpose(total[:up]),
            jnp.transpose(total[up : up + out]),
            jnp.transpose(jnp.concatenate([x for x in down], axis=1)),
        )

    def by_plane(x, which):
        return lax.dynamic_index_in_dim(x.reshape((outers, INNER) + x.shape[1:]), which, 1, False)

    def to_planes():
        arrived = []
        for flip in (1, 2, 3):
            pairs = [(r, r ^ flip) for r in range(row_size)]
            arrived.append(lax.ppermute(by_plane(ffn_grads, inner ^ flip), "row", pairs))
        return arrived

    def plane_sums(arrived):
        total = by_plane(ffn_grads, inner).astype(f32)
        for some in arrived:
            total = total + some.astype(f32)
        own = lax.dynamic_index_in_dim(total, outer, 0, False)
        others = [
            lax.dynamic_index_in_dim(total, (outer + step) % outers, 0, False).astype(bf16)
            for step in range(1, outers)
        ]
        return own, others

    def to_columns(others):
        arrived = []
        for step in range(1, outers):
            pairs = [
                (r, ((r // INNER + step) % outers) * INNER + r % INNER) for r in range(row_size)
            ]
            arrived.append(lax.ppermute(others[step - 1], "row", pairs))
        return arrived

    def over_rows(x):
        return jnp.transpose(
            lax.psum_scatter(x, "row", scatter_dimension=0, tiled=False).astype(f32)
        )

    do_wide = padded(grad_att_low, 1)
    do_wide, ffn_grads = lax.optimization_barrier((do_wide, ffn_grads))
    if dealt:
        arrived = to_planes()
    else:
        summed = lax.psum_scatter(ffn_grads, "row", scatter_dimension=0, tiled=False).astype(f32)

    dq, dkt, dvt, pair_t, kernel_sums = attention_backward(
        lo, hi, probs, inverse_total, queries, do_wide, att_wide, keys, values_t,
        qpos, kpos, cen, amp, lnorm, w_pair, head_dim,
    )
    if dealt:
        dq, arrived = lax.optimization_barrier((dq, arrived))
        own_sum, others = plane_sums(arrived)
        dq, others = lax.optimization_barrier((dq, others))
        far_sums = to_columns(others)
        grad_normed_in, w_qkv_grad_t = finish_rows(
            dkt, dvt, dq, every, normed_in, w_q, w_qkv_full, row_size, head_dim
        )
        grad_normed_in, far_sums = lax.optimization_barrier((grad_normed_in, far_sums))
        summed = own_sum + sum(x.astype(f32) for x in far_sums)
        w_qkv_grad = jnp.transpose(w_qkv_grad_t)
    else:
        key_grad, value_grad = jnp.transpose(dkt), jnp.transpose(dvt)
        grad_every = along_rows(key_grad, w_qkv_full[:, model_width : 2 * model_width])
        grad_every += along_rows(value_grad, w_qkv_full[:, 2 * model_width :])
        grad_normed_in = along_rows(dq, w_q) + send_back(grad_every)
        whole_grad = jnp.concatenate(
            [
                unpadded(cross_rows(dq, normed_in), 0),
                cross_rows(key_grad, every),
                cross_rows(value_grad, every),
            ],
            axis=0,
        ).astype(bf16)
        half_grad = lax.psum_scatter(whole_grad, "wt", scatter_dimension=1, tiled=True)
        w_qkv_grad = over_rows(half_grad.reshape(row_size, -1, half_grad.shape[1]))
    w_up_grad, w_out_grad, w_down_grad = split_grads(summed)
    grad_norm_one, grad_gain_one, grad_shift_one = norm_back(
        grad_normed_in, normed_one, inverse_one, gain_one
    )
    atoms_grad = grad_after + grad_norm_one
    grad_table = lax.dot_general(
        onehot.astype(f32),
        atoms_grad,
        (((0,), (0,)), ((), ())),
        precision=HIGHEST,
        preferred_element_type=f32,
    )
    sums = jnp.sum(kernel_sums, axis=2)
    center_part = sums[1] / (steep * widths)
    width_part = (sums[2] / (steep * steep) - sums[0]) / widths
    small = (
        grad_table,
        grad_gain_one,
        grad_shift_one,
        center_part,
        width_part,
        jnp.transpose(pair_t),
        grad_gain_two,
        grad_shift_two,
        grad_force,
    )
    if dealt:
        flat = jnp.concatenate([x.reshape(-1) for x in small])
        devices = row_size * lax.axis_size("wt")
        piece = -(-flat.shape[0] // (devices * 8 * 128)) * 128
        flat = jnp.pad(flat, (0, devices * 8 * piece - flat.shape[0]))
        flat, atoms_grad, out_low, forces_in = total_over_all(
            flat.reshape(devices, 8, piece),
            quarters(atoms_grad),
            quarters(out_low),
            jnp.pad(force_rows, ((0, 5), (0, 0))),
        )
        flat = flat.reshape(-1)
        atoms_grad = atoms_grad.reshape(row_count, model_width)
        out_low = out_low.reshape(row_count, model_width)
        forces_in = lax.dynamic_slice_in_dim(forces_in[:, :3, :], outer * QB, QB, 2)
        force_rows = jnp.swapaxes(forces_in, 0, 1).reshape(3, row_count)
        small_sums, at = [], 0
        for x in small:
            small_sums.append(flat[at : at + x.size].reshape(x.shape))
            at += x.size
    else:
        small_sums = lax.psum(small, ("row", "wt"))
    return (
        out_low[None],
        force_rows[:, None, :],
        atoms_grad[None],
        small_sums[0],
        small_sums[1],
        small_sums[2],
        w_qkv_grad,
        small_sums[3],
        small_sums[4],
        small_sums[5],
        w_out_grad,
        small_sums[6],
        small_sums[7],
        w_up_grad,
        w_down_grad,
        small_sums[8],
    )


def solution(mesh):
    in_specs = (
        P("wt", "row", None),
        P(None, "wt", "row"),
        P("wt", "row"),
        P("wt", None),
        P("wt"),
        P(),
        P(),
        P(),
        P("wt", None),
        P(),
        P(),
        P(),
        P("wt", None),
        P(),
        P(),
        P("wt", None),
        P("wt", None),
        P(),
        P("wt", "row", None),
        P(None, "wt", "row"),
    )
    out_specs = (
        P("wt", "row", None),
        P(None, "wt", "row"),
        P("wt", "row", None),
        P(),
        P(),
        P(),
        P("wt", "row"),
        P(),
        P(),
        P(),
        P("wt", "row"),
        P(),
        P(),
        P("wt", "row"),
        P("wt", "row"),
        P(),
    )
    return jax.shard_map(
        on_device, mesh=mesh, in_specs=in_specs, out_specs=out_specs, check_vma=False
    )
```
